256 devices in a mesh: row: 8 (over y, core), col: 32 (over x, z).
Axes of the slice: x: 4, y: 4, z: 8, core: 2. Of those that a mesh axis runs over, the one named last changes fastest.
Arguments:
- kkt: float32 [8192, 8192], P('row', 'col'), may hold values from -4 to 4, as said below
- swaps: int32 [2, 2, 128], replicated, may hold values from 0 to 8191, as said below
- inverses: float32 [2, 256, 256], replicated
- pivots: float32 [2, 256], replicated, may hold values from -0.12 to 0.12
- couplings: float32 [2, 256], replicated, may hold values from -0.12 to 0.12
- pattern: int32 [2, 256], replicated, may hold values from 0 to 1, as said below
Outputs:
- factored: float32 [8192, 8192], P('row', 'col')
The draws below stay inside these ranges and needn't reach their ends.
Inputs may be any that keep to these rules, and one draw needn't show every extreme that they name: For panel k, swaps[k, 0, :] holds 128 distinct rows among k * 256 to k * 256 + 255, both ends of that range among them, and swaps[k, 1, :] holds 128 distinct rows among (k + 1) * 256 to 8191, both ends of that range among them. pattern[k, i] = 1 makes rows i and i + 1 one 2 x 2 block of D; no two neighbouring entries are both 1 and the last entry is 0. kkt is the stored order of a symmetric matrix.
All inputs are finite; a program needn't handle non-finite values.
Results may differ from the reference program's by a relative error of at most 0.00014.
Values sent between devices are 32-bit elements; how exact they have to be, the bound alone decides.
A program may use at most 64 MiB of HBM per device.

```python
import math
import jax
import jax.numpy as jnp
from jax import lax

NB = 256
SW = 128
T_COL = 1
T_ROW = 4
N = 8192


def stored_to_global_drawn(total, tiles_dev, tile_width):
    group_total = total // (tiles_dev * tile_width)
    positions = jnp.arange(total, dtype=jnp.int32)
    tile_idx = positions // tile_width
    return (tile_idx % tiles_dev * group_total + tile_idx // tiles_dev) * tile_width + positions % tile_width


def draw_kkt(key, part):
    noise_field = jnp.clip(jax.random.normal(key, (N, N), jnp.float32), -4.0, 4.0)
    symmetric = jnp.triu(noise_field) + jnp.triu(noise_field, 1).T
    row_map = stored_to_global_drawn(N, T_ROW, NB)
    col_map = stored_to_global_drawn(N, T_COL, NB)
    return jnp.take(jnp.take(symmetric, row_map, axis=0), col_map, axis=1)


def pick_distinct(key, span, amount):
    inner = jax.random.permutation(key, span - 2)[:amount - 2].astype(jnp.int32) + 1
    chosen = jnp.concatenate([jnp.array([0, span - 1], jnp.int32), inner])
    shuffle = jax.random.permutation(jax.random.fold_in(key, 7), amount)
    return jnp.take(chosen, shuffle)


def draw_swaps(key, part):
    panels = []
    for panel in range(2):
        lead_rows = panel * NB + pick_distinct(jax.random.fold_in(key, 10 + panel), NB, SW)
        partner_rows = (panel + 1) * NB + pick_distinct(jax.random.fold_in(key, 20 + panel), N - (panel + 1) * NB, SW)
        panels.append(jnp.stack([lead_rows, partner_rows]))
    return jnp.stack(panels).astype(jnp.int32)


def draw_pattern(key, part):
    coin_flips = jax.random.randint(key, (2, NB), 0, 2, dtype=jnp.int32)
    coin_flips = coin_flips.at[:, 0].set(1).at[:, NB - 1].set(0)

    def advance(earlier, flip):
        marked = flip * (1 - earlier)
        return (marked, marked)
    _, marks = lax.scan(advance, jnp.zeros((2,), jnp.int32), coin_flips.T)
    return marks.T


def draw_inverses(key, part):
    noise_field = jnp.clip(jax.random.normal(key, (2, NB, NB), jnp.float32), -4.0, 4.0)
    return jnp.eye(NB, dtype=jnp.float32)[None, :, :] + noise_field * (0.5 / math.sqrt(NB))


def setup_inputs(seed: int = 0) -> dict:
    key_list = jax.random.split(jax.random.key(seed), 7)
    return {
        "kkt": draw_kkt(jax.random.fold_in(key_list[6], 71), 0),
        "swaps": draw_swaps(jax.random.fold_in(key_list[6], 71), 0),
        "inverses": draw_inverses(jax.random.fold_in(key_list[6], 71), 0),
        "pivots": jnp.clip(jax.random.uniform(key_list[3], (2, NB), jnp.float32, -0.12, 0.12), -0.12, 0.12),
        "couplings": jnp.clip(jax.random.uniform(key_list[4], (2, NB), jnp.float32, -0.12, 0.12), -0.12, 0.12),
        "pattern": draw_pattern(jax.random.fold_in(key_list[6], 71), 0),
    }


highest_prec = lax.Precision.HIGHEST


def stored_to_global(total, tiles_dev, tile_width):
    group_total = total // (tiles_dev * tile_width)
    positions = jnp.arange(total, dtype=jnp.int32)
    tile_idx = positions // tile_width
    return ((tile_idx % tiles_dev) * group_total + tile_idx // tiles_dev) * tile_width + positions % tile_width


def global_to_stored(total, tiles_dev, tile_width):
    group_total = total // (tiles_dev * tile_width)
    positions = jnp.arange(total, dtype=jnp.int32)
    tile_idx = positions // tile_width
    return ((tile_idx % group_total) * tiles_dev + tile_idx // group_total) * tile_width + positions % tile_width


def swap_order(lead_rows, partner_rows, total):
    row_order = jnp.arange(total, dtype=jnp.int32)
    return row_order.at[lead_rows].set(partner_rows).at[partner_rows].set(lead_rows)


def scale_cols(lower_rows, pivot_row, coupling_row, pattern_row):
    links = coupling_row * pattern_row.astype(jnp.float32)
    zero_col = jnp.zeros((lower_rows.shape[0], 1), lower_rows.dtype)
    after = jnp.concatenate([lower_rows[:, 1:], zero_col], axis=1)
    before = jnp.concatenate([zero_col, lower_rows[:, :-1]], axis=1)
    links_before = jnp.concatenate([jnp.zeros((1,), links.dtype), links[:-1]])
    return lower_rows * pivot_row + after * links + before * links_before


def reference(kkt, swaps, inverses, pivots, couplings, pattern):
    row_map = global_to_stored(N, T_ROW, NB)
    col_map = global_to_stored(N, T_COL, NB)
    matrix = jnp.take(jnp.take(kkt, row_map, axis=0), col_map, axis=1)
    tile_of = jnp.arange(N, dtype=jnp.int32) // NB
    for panel in range(2):
        row_order = swap_order(swaps[panel, 0], swaps[panel, 1], N)
        matrix = jnp.take(jnp.take(matrix, row_order, axis=0), row_order, axis=1)
        trailing = (tile_of > panel)[:, None]
        product = jnp.dot(matrix[:, panel * NB:(panel + 1) * NB], inverses[panel], precision=highest_prec, preferred_element_type=jnp.float32)
        lower_rows = jnp.where(trailing, product, 0.0)
        scaled = scale_cols(lower_rows, pivots[panel], couplings[panel], pattern[panel])
        matrix = matrix - jnp.dot(lower_rows, scaled.T, precision=highest_prec, preferred_element_type=jnp.float32)
        panel_block = jnp.where(trailing, lower_rows, matrix[:, panel * NB:(panel + 1) * NB])
        matrix = matrix.at[:, panel * NB:(panel + 1) * NB].set(panel_block)
        top_block = jnp.where(trailing.T, scaled.T, matrix[panel * NB:(panel + 1) * NB, :])
        matrix = matrix.at[panel * NB:(panel + 1) * NB, :].set(top_block)
    back_rows = stored_to_global(N, T_ROW, NB)
    back_cols = stored_to_global(N, T_COL, NB)
    return jnp.take(jnp.take(matrix, back_rows, axis=0), back_cols, axis=1)
```

```python
import jax
import jax.numpy as jnp
from jax import lax
from jax.sharding import Mesh
from jax.sharding import PartitionSpec as P

COL = ("col_0", "col_1")
HI = lax.Precision.HIGHEST


def tdot(a, b):
    return lax.dot_general(
        a, b, (((0,), (0,)), ((), ())), precision=HI, preferred_element_type=jnp.float32
    )


def swapped(rows, lead, partner):
    to_partner = rows[:, None] == lead[None, :]
    to_lead = rows[:, None] == partner[None, :]
    moved = jnp.sum(
        jnp.where(to_partner, partner[None, :], 0) + jnp.where(to_lead, lead[None, :], 0), axis=1
    )
    return jnp.where(jnp.any(to_partner | to_lead, axis=1), moved, rows)


def plan(swaps, tile, row_groups, dtype=jnp.float32):
    width = tile // row_groups
    count = swaps.shape[2]
    partner = swaps[:, 1, :].reshape(-1)
    top = jnp.arange(2 * tile, dtype=jnp.int32)
    rows = jnp.concatenate([top, partner])
    source = swapped(swapped(rows, swaps[1, 0], swaps[1, 1]), swaps[0, 0], swaps[0, 1])
    repeated = jnp.any(swaps[0, 1][:, None] == swaps[1, 1][None, :], axis=1)
    valid = jnp.concatenate([~repeated, jnp.ones((count,), bool)]) & (partner >= 2 * tile)
    sliced = source.reshape(3, row_groups, width).transpose(1, 0, 2)
    return rows, source, sliced, jnp.where(valid, partner, -1)


def hits(rows, first, tile):
    return (rows[:, None] == first + jnp.arange(tile, dtype=jnp.int32)[None, :]).astype(jnp.float32)


def along_d(lower_t, pivot, coupling, pattern):
    links = coupling * pattern.astype(jnp.float32)
    zero = jnp.zeros((1, lower_t.shape[1]), lower_t.dtype)
    after = jnp.concatenate([lower_t[1:], zero], axis=0)
    before = jnp.concatenate([zero, lower_t[:-1]], axis=0)
    links_before = jnp.concatenate([jnp.zeros((1,), links.dtype), links[:-1]])
    return lower_t * pivot[:, None] + after * links[:, None] + before * links_before[:, None]


def exchange(picked, moves, tile, row_groups, x_size):
    width = tile // row_groups
    row_index = lax.axis_index("row")
    z_index = lax.axis_index("col_1")
    piece = lax.psum_scatter(picked, "row", scatter_dimension=0, tiled=False)
    strip = lax.all_gather(piece, "row")
    mine = lax.psum(jnp.where(z_index == row_index, strip, 0.0), "col_1")
    wide = lax.all_gather(mine, "col_0")
    part = jnp.dot(piece, moves, precision=HI, preferred_element_type=jnp.float32)
    t0, t1, tp = part[:width], part[width : 2 * width], part[2 * width :]
    corner = jnp.stack(
        [
            t0[:, 2 * tile :],
            t1[:, 2 * tile :],
            tp[:, 2 * tile :],
            t0[:, tile : 2 * tile],
            t0[:, :tile],
            t1[:, tile : 2 * tile],
        ]
    )
    corner = lax.all_gather(lax.psum(corner, COL), "row")
    return strip, wide, corner


def shards(kkt, swaps, inverses, pivots, couplings, pattern):
    tile = inverses.shape[1]
    row_groups = lax.axis_size("row")
    x_size = lax.axis_size("col_0")
    z_size = lax.axis_size("col_1")
    row_index = lax.axis_index("row")
    col_index = lax.axis_index(COL)
    rows, source, sliced, partner = plan(swaps, tile, row_groups)
    flat = sliced.reshape(-1)
    owned = flat // tile % row_groups == row_index
    taken = jnp.take(kkt, flat // tile // row_groups * tile + flat % tile, axis=0)
    picked = jnp.where(owned[:, None], taken, 0.0).reshape(row_groups, -1, tile)
    moves = hits(source, col_index * tile, tile).T
    strip, wide, corner = exchange(picked, moves, tile, row_groups, x_size)

    def ordered(piece):
        return piece.reshape(row_groups, 3, -1, tile).transpose(1, 0, 2, 3).reshape(-1, tile)

    corner = corner.transpose(1, 0, 2, 3).reshape(6, tile, tile)
    to_partner = corner[0:3].reshape(3 * tile, tile)
    block_01, block_00, block_11 = corner[3], corner[4], corner[5]

    tiles = [row_index + row_groups * slot for slot in range(x_size)] + [col_index]
    strips = [ordered(wide[slot]) for slot in range(x_size)] + [ordered(strip)]
    marks = [hits(partner, index * tile, tile) for index in tiles]
    keep = [1.0 - jnp.sum(mark, axis=0) for mark in marks]
    fixed = [
        strips[n] * keep[n][None, :]
        + jnp.dot(to_partner, marks[n], precision=HI, preferred_element_type=jnp.float32)
        for n in range(x_size + 1)
    ]
    upper = [jnp.where(tiles[n] == 1, block_01, fixed[n][:tile]) for n in range(x_size + 1)]
    low0 = [jnp.where(tiles[n] > 0, tdot(inverses[0], upper[n]), 0.0) for n in range(x_size + 1)]
    low0_1 = tdot(inverses[0], block_01)
    scaled0_1 = along_d(low0_1, pivots[0], couplings[0], pattern[0])
    scaled0 = along_d(low0[-1], pivots[0], couplings[0], pattern[0])
    low1 = [
        jnp.where(
            tiles[n] > 1,
            tdot(inverses[1], fixed[n][tile : 2 * tile] - tdot(scaled0_1, low0[n])),
            0.0,
        )
        for n in range(x_size + 1)
    ]
    scaled1 = along_d(low1[-1], pivots[1], couplings[1], pattern[1])
    outs = []
    for n in range(x_size):
        base = kkt[n * tile : (n + 1) * tile] * keep[n][:, None] * keep[-1][None, :]
        base = base + tdot(marks[n], fixed[-1][2 * tile :])
        base = base + tdot(fixed[n][2 * tile :] * keep[n][None, :], marks[-1])
        value = base - tdot(low0[n], scaled0) - tdot(low1[n], scaled1)
        value = jnp.where(tiles[n] == 0, scaled0, value)
        value = jnp.where(tiles[n] == 1, scaled1, value)
        at_0 = jnp.where(tiles[n] == 0, block_00, low0[n].T)
        at_1 = jnp.where(tiles[n] == 0, scaled0_1, low1[n].T)
        at_1 = jnp.where(tiles[n] == 1, block_11 - tdot(low0_1, scaled0_1), at_1)
        value = jnp.where(col_index == 0, at_0, value)
        value = jnp.where(col_index == 1, at_1, value)
        outs.append(value)
    return jnp.concatenate(outs, axis=0)


def solution(mesh):
    z_size = mesh.shape["row"]
    finer = Mesh(mesh.devices.reshape(mesh.shape["row"], -1, z_size), ("row", "col_0", "col_1"))
    in_specs = (P("row", COL), P(), P(), P(), P(), P())
    return jax.shard_map(
        shards, mesh=finer, in_specs=in_specs, out_specs=P("row", COL), check_vma=False
    )
```

```python
import functools

import jax
import jax.numpy as jnp
from jax import lax
from jax.experimental import pallas as pl
from jax.experimental.pallas import tpu as pltpu
from jax.sharding import Mesh
from jax.sharding import PartitionSpec as P

COL = ("col_0", "col_1")
HI = lax.Precision.HIGHEST


def tdot(a, b):
    return lax.dot_general(
        a, b, (((0,), (0,)), ((), ())), precision=HI, preferred_element_type=jnp.float32
    )


def swapped(rows, lead, partner):
    to_partner = rows[:, None] == lead[None, :]
    to_lead = rows[:, None] == partner[None, :]
    moved = jnp.sum(
        jnp.where(to_partner, partner[None, :], 0) + jnp.where(to_lead, lead[None, :], 0), axis=1
    )
    return jnp.where(jnp.any(to_partner | to_lead, axis=1), moved, rows)


def plan(swaps, tile, row_groups, dtype=jnp.float32):
    width = tile // row_groups
    count = swaps.shape[2]
    partner = swaps[:, 1, :].reshape(-1)
    top = jnp.arange(2 * tile, dtype=jnp.int32)
    rows = jnp.concatenate([top, partner])
    source = swapped(swapped(rows, swaps[1, 0], swaps[1, 1]), swaps[0, 0], swaps[0, 1])
    repeated = jnp.any(swaps[0, 1][:, None] == swaps[1, 1][None, :], axis=1)
    valid = jnp.concatenate([~repeated, jnp.ones((count,), bool)]) & (partner >= 2 * tile)
    sliced = source.reshape(3, row_groups, width).transpose(1, 0, 2)
    return rows, source, sliced, jnp.where(valid, partner, -1)


def hits(rows, first, tile):
    return (rows[:, None] == first + jnp.arange(tile, dtype=jnp.int32)[None, :]).astype(jnp.float32)


def along_d(lower_t, pivot, coupling, pattern):
    links = coupling * pattern.astype(jnp.float32)
    zero = jnp.zeros((1, lower_t.shape[1]), lower_t.dtype)
    after = jnp.concatenate([lower_t[1:], zero], axis=0)
    before = jnp.concatenate([zero, lower_t[:-1]], axis=0)
    links_before = jnp.concatenate([jnp.zeros((1,), links.dtype), links[:-1]])
    return lower_t * pivot[:, None] + after * links[:, None] + before * links_before[:, None]


MESH = pl.DeviceIdType.MESH


def remote(src, dst, send, recv, device):
    return pltpu.make_async_remote_copy(
        src_ref=src, dst_ref=dst, send_sem=send, recv_sem=recv, device_id=device, device_id_type=MESH
    )


def exchange_kernel(
    sizes,
    picked,
    moves,
    strip,
    wide,
    corner,
    special,
    arrived,
    shares,
    share,
    share_in,
    cross,
    summed,
    rs_send,
    rs_recv,
    ag_send,
    ag_recv,
    z_send,
    z_recv,
    x_send,
    x_recv,
    f_send,
    f_recv,
    cz_send,
    cz_recv,
    cx_send,
    cx_recv,
    cg_send,
    cg_recv,
    cr_send,
    cr_recv,
    sp_send,
    sp_recv,
):
    rows_n, x_n, z_n, width = sizes
    r = lax.axis_index("row")
    x = lax.axis_index("col_0")
    z = lax.axis_index("col_1")

    def row_peer(d):
        return (lax.rem(r + d, rows_n), x, z)

    def z_peer(d):
        return (r, x, lax.rem(z + d + z_n, z_n))

    def x_peer(d):
        return (r, lax.rem(x + d + x_n, x_n), z)

    barrier = pltpu.get_barrier_semaphore()
    for d in range(1, rows_n):
        pl.semaphore_signal(barrier, inc=1, device_id=row_peer(d), device_id_type=MESH)
    for d in range(1, z_n):
        pl.semaphore_signal(barrier, inc=1, device_id=z_peer(d), device_id_type=MESH)
    for d in range(1, x_n):
        pl.semaphore_signal(barrier, inc=1, device_id=x_peer(d), device_id_type=MESH)
    pl.semaphore_wait(barrier, rows_n + z_n + x_n - 3)

    def reduce_copy(d):
        return remote(
            picked.at[lax.rem(r + d, rows_n)],
            arrived.at[d - 1],
            rs_send.at[d - 1],
            rs_recv.at[d - 1],
            row_peer(d),
        )

    for d in range(1, rows_n):
        reduce_copy(d).start()
    total = picked[r]
    for d in range(1, rows_n):
        reduce_copy(d).wait_recv()
        total = total + arrived[d - 1]
    strip[r] = total

    def gather_copy(d):
        return remote(
            strip.at[r], strip.at[r], ag_send.at[d - 1], ag_recv.at[d - 1], row_peer(d)
        )

    def gathered(d):
        q = lax.rem(r - d + rows_n, rows_n)
        return remote(
            strip.at[q], strip.at[q], ag_send.at[d - 1], ag_recv.at[d - 1], row_peer(d)
        )

    for d in range(1, rows_n):
        gather_copy(d).start()

    offset = lax.rem(z - r + z_n, z_n)
    half = z_n // 2
    is_root = offset == 0
    upward = offset <= half
    passes = ((offset > 0) & (offset < half)) | (offset > half + 1)
    ahead = jnp.where(upward, 1, z_n - 1)

    def z_copy(src, q, d, slot, step):
        return remote(
            src, wide.at[x, q], z_send.at[slot, d], z_recv.at[d], z_peer(step)
        )

    def x_copy(src, q, d, side):
        return remote(
            src,
            wide.at[x, q],
            x_send.at[side, d],
            x_recv.at[side, d],
            x_peer(1 if side == 0 else x_n - 1),
        )

    def f_copy(d, q):
        if d % 2 == 0:
            held = wide.at[lax.rem(x + x_n - 1, x_n), q]
            return remote(held, held, f_send.at[d], f_recv.at[d], x_peer(1))
        held = wide.at[lax.rem(x + 1, x_n), q]
        return remote(held, held, f_send.at[d], f_recv.at[d], x_peer(x_n - 1))

    def own_piece(d):
        q = lax.rem(r - d + rows_n, rows_n)

        @pl.when(is_root)
        def _():
            if d > 0:
                gathered(d).wait_recv()
            z_copy(strip.at[q], q, d, 0, 1).start()
            z_copy(strip.at[q], q, d, 1, z_n - 1).start()
            x_copy(strip.at[q], q, d, 0).start()
            x_copy(strip.at[q], q, d, 1).start()
            wide[x, q] = strip[q]

        @pl.when(jnp.logical_not(is_root))
        def _():
            z_copy(wide.at[x, q], q, d, 0, ahead).wait_recv()

            @pl.when(passes)
            def _():
                z_copy(wide.at[x, q], q, d, 0, ahead).start()

            x_copy(wide.at[x, q], q, d, 0).start()
            x_copy(wide.at[x, q], q, d, 1).start()

    def side_piece(d):
        q = lax.rem(r - d + rows_n, rows_n)
        x_copy(wide.at[x, q], q, d, 0).wait_recv()
        if d % 2 == 0:
            f_copy(d, q).start()
        x_copy(wide.at[x, q], q, d, 1).wait_recv()
        if d % 2 == 1:
            f_copy(d, q).start()

    def share_copy(d):
        return remote(
            shares.at[lax.rem(z + d, z_n)],
            share_in.at[d - 1],
            cz_send.at[d - 1],
            cz_recv.at[d - 1],
            z_peer(d),
        )

    def cross_copy(d):
        return remote(share, cross.at[d - 1], cx_send.at[d - 1], cx_recv.at[d - 1], x_peer(d))

    def share_back(d):
        return remote(
            summed.at[z], summed.at[z], cg_send.at[d - 1], cg_recv.at[d - 1], z_peer(d)
        )

    def share_taken(d):
        q = lax.rem(z - d + z_n, z_n)
        return remote(
            summed.at[q], summed.at[q], cg_send.at[d - 1], cg_recv.at[d - 1], z_peer(d)
        )

    own_piece(0)

    part = jnp.dot(
        strip[r], moves[...], precision=HI, preferred_element_type=jnp.float32
    )
    tile = moves.shape[1] // 3
    blocks = (
        (0, 2), (1, 2), (2, 2), (0, 1), (0, 0), (1, 1)
    )
    stacked = jnp.concatenate(
        [
            part[i * width : (i + 1) * width, j * tile : (j + 1) * tile]
            for i, j in blocks
        ],
        axis=0,
    )
    depth = 6 * width // z_n
    for n in range(z_n):
        shares[n] = stacked[n * depth : (n + 1) * depth]
    for d in range(1, z_n):
        share_copy(d).start()

    own_piece(1)
    side_piece(0)
    own_piece(2)
    side_piece(1)

    value = shares[z]
    for d in range(1, z_n):
        share_copy(d).wait_recv()
        value = value + share_in[d - 1]
    share[...] = value
    for d in range(1, x_n):
        cross_copy(d).start()

    if rows_n > 4:
        own_piece(3)
        side_piece(2)
    for d in range(1, x_n):
        cross_copy(d).wait_recv()
        value = value + cross[d - 1]
    summed[z] = value
    for d in range(1, z_n):
        share_back(d).start()

    first = 4 if rows_n > 4 else 3
    for d in range(first, rows_n):
        own_piece(d)
        side_piece(d - 1)
        if d == rows_n - 2 or rows_n == 4:
            for e in range(1, z_n):
                share_taken(e).wait_recv()
            flat = jnp.concatenate([summed[n] for n in range(z_n)], axis=0)
            corner[r] = flat[: 4 * width]
            special[r] = flat[4 * width :]
            for e in range(1, rows_n):
                remote(
                    corner.at[r], corner.at[r], cr_send.at[e - 1], cr_recv.at[e - 1], row_peer(e)
                ).start()
            for home in range(2):
                @pl.when((x == 0) & (z == home) & (r != home))
                def _():
                    remote(
                        special.at[r],
                        special.at[r],
                        sp_send,
                        sp_recv.at[r],
                        (home, x, z),
                    ).start()
    side_piece(rows_n - 1)

    for d in range(1, rows_n):
        @pl.when(jnp.logical_not(is_root))
        def _():
            gathered(d).wait_recv()

        q = lax.rem(r - d + rows_n, rows_n)
        remote(
            corner.at[q], corner.at[q], cr_send.at[d - 1], cr_recv.at[d - 1], row_peer(d)
        ).wait()
        reduce_copy(d).wait_send()
        gather_copy(d).wait_send()
    for d in range(rows_n):
        q = lax.rem(r - d + rows_n, rows_n)
        f_copy(d, q).wait()
        x_copy(wide.at[x, q], q, d, 0).wait_send()
        x_copy(wide.at[x, q], q, d, 1).wait_send()

        @pl.when(is_root | passes)
        def _():
            z_copy(wide.at[x, q], q, d, 0, ahead).wait_send()

        @pl.when(is_root)
        def _():
            z_copy(wide.at[x, q], q, d, 1, ahead).wait_send()

    for d in range(1, z_n):
        share_copy(d).wait_send()
        share_back(d).wait_send()
    for d in range(1, x_n):
        cross_copy(d).wait_send()
    for home in range(2):
        for n in range(rows_n):
            if n != home:
                here = (x == 0) & (z == home)

                @pl.when(here & (r == n))
                def _():
                    remote(
                        special.at[n], special.at[n], sp_send, sp_recv.at[n], (home, x, z)
                    ).wait_send()

                @pl.when(here & (r == home))
                def _():
                    remote(
                        special.at[n], special.at[n], sp_send, sp_recv.at[n], (n, x, z)
                    ).wait_recv()


def exchange(picked, moves, tile, rows_n, x_n):
    z_n = rows_n
    width = tile // rows_n
    depth = 6 * width // z_n
    f32 = jnp.float32
    dma = pltpu.SemaphoreType.DMA
    vmem = pl.BlockSpec(memory_space=pltpu.VMEM)
    return pl.pallas_call(
        functools.partial(exchange_kernel, (rows_n, x_n, z_n, width)),
        out_shape=(
            jax.ShapeDtypeStruct((rows_n, 3 * width, tile), f32),
            jax.ShapeDtypeStruct((x_n, rows_n, 3 * width, tile), f32),
            jax.ShapeDtypeStruct((rows_n, 4 * width, tile), f32),
            jax.ShapeDtypeStruct((rows_n, 2 * width, tile), f32),
        ),
        in_specs=[vmem] * 2,
        out_specs=(vmem,) * 4,
        scratch_shapes=[
            pltpu.VMEM((rows_n - 1, 3 * width, tile), f32),
            pltpu.VMEM((z_n, depth, tile), f32),
            pltpu.VMEM((depth, tile), f32),
            pltpu.VMEM((z_n - 1, depth, tile), f32),
            pltpu.VMEM((x_n - 1, depth, tile), f32),
            pltpu.VMEM((z_n, depth, tile), f32),
            dma((rows_n - 1,)),
            dma((rows_n - 1,)),
            dma((rows_n - 1,)),
            dma((rows_n - 1,)),
            dma((2, rows_n)),
            dma((rows_n,)),
            dma((2, rows_n)),
            dma((2, rows_n)),
            dma((rows_n,)),
            dma((rows_n,)),
            dma((z_n - 1,)),
            dma((z_n - 1,)),
            dma((x_n - 1,)),
            dma((x_n - 1,)),
            dma((z_n - 1,)),
            dma((z_n - 1,)),
            dma((rows_n - 1,)),
            dma((rows_n - 1,)),
            dma,
            dma((rows_n,)),
        ],
        compiler_params=pltpu.CompilerParams(collective_id=0, has_side_effects=True),
    )(picked, moves)


def shards(kkt, swaps, inverses, pivots, couplings, pattern):
    tile = inverses.shape[1]
    row_groups = lax.axis_size("row")
    x_size = lax.axis_size("col_0")
    z_size = lax.axis_size("col_1")
    row_index = lax.axis_index("row")
    col_index = lax.axis_index(COL)
    rows, source, sliced, partner = plan(swaps, tile, row_groups)
    flat = sliced.reshape(-1)
    owned = flat // tile % row_groups == row_index
    taken = jnp.take(kkt, flat // tile // row_groups * tile + flat % tile, axis=0)
    picked = jnp.where(owned[:, None], taken, 0.0).reshape(row_groups, -1, tile)
    moves = hits(source, col_index * tile, tile).T
    strip, wide, corner, special = exchange(picked, moves, tile, row_groups, x_size)

    def ordered(piece):
        return piece.reshape(row_groups, 3, -1, tile).transpose(1, 0, 2, 3).reshape(-1, tile)

    corner = corner.reshape(row_groups, 4, -1, tile).transpose(1, 0, 2, 3).reshape(4, tile, tile)
    special = special.reshape(row_groups, 2, -1, tile).transpose(1, 0, 2, 3).reshape(2, tile, tile)
    to_partner = corner[0:3].reshape(3 * tile, tile)
    block_01, block_00, block_11 = corner[3], special[0], special[1]

    tiles = [row_index + row_groups * slot for slot in range(x_size)] + [col_index]
    strips = [ordered(wide[slot]) for slot in range(x_size)] + [ordered(strip)]
    marks = [hits(partner, index * tile, tile) for index in tiles]
    keep = [1.0 - jnp.sum(mark, axis=0) for mark in marks]
    fixed = [
        strips[n] * keep[n][None, :]
        + jnp.dot(to_partner, marks[n], precision=HI, preferred_element_type=jnp.float32)
        for n in range(x_size + 1)
    ]
    upper = [jnp.where(tiles[n] == 1, block_01, fixed[n][:tile]) for n in range(x_size + 1)]
    low0 = [jnp.where(tiles[n] > 0, tdot(inverses[0], upper[n]), 0.0) for n in range(x_size + 1)]
    low0_1 = tdot(inverses[0], block_01)
    scaled0_1 = along_d(low0_1, pivots[0], couplings[0], pattern[0])
    scaled0 = along_d(low0[-1], pivots[0], couplings[0], pattern[0])
    low1 = [
        jnp.where(
            tiles[n] > 1,
            tdot(inverses[1], fixed[n][tile : 2 * tile] - tdot(scaled0_1, low0[n])),
            0.0,
        )
        for n in range(x_size + 1)
    ]
    scaled1 = along_d(low1[-1], pivots[1], couplings[1], pattern[1])
    outs = []
    for n in range(x_size):
        base = kkt[n * tile : (n + 1) * tile] * keep[n][:, None] * keep[-1][None, :]
        base = base + tdot(marks[n], fixed[-1][2 * tile :])
        base = base + tdot(fixed[n][2 * tile :] * keep[n][None, :], marks[-1])
        value = base - tdot(low0[n], scaled0) - tdot(low1[n], scaled1)
        value = jnp.where(tiles[n] == 0, scaled0, value)
        value = jnp.where(tiles[n] == 1, scaled1, value)
        at_0 = jnp.where(tiles[n] == 0, block_00, low0[n].T)
        at_1 = jnp.where(tiles[n] == 0, scaled0_1, low1[n].T)
        at_1 = jnp.where(tiles[n] == 1, block_11 - tdot(low0_1, scaled0_1), at_1)
        value = jnp.where(col_index == 0, at_0, value)
        value = jnp.where(col_index == 1, at_1, value)
        outs.append(value)
    return jnp.concatenate(outs, axis=0)


def solution(mesh):
    z_size = mesh.shape["row"]
    finer = Mesh(mesh.devices.reshape(mesh.shape["row"], -1, z_size), ("row", "col_0", "col_1"))
    in_specs = (P("row", COL), P(), P(), P(), P(), P())
    return jax.shard_map(
        shards, mesh=finer, in_specs=in_specs, out_specs=P("row", COL), check_vma=False
    )
```

```python
import functools

import jax
import jax.numpy as jnp
from jax import lax
from jax.experimental import pallas as pl
from jax.experimental.pallas import tpu as pltpu
from jax.sharding import Mesh
from jax.sharding import PartitionSpec as P

COL = ("col_0", "col_1")
HI = lax.Precision.HIGHEST


def swapped(rows, lead, partner):
    to_partner = rows[:, None] == lead[None, :]
    to_lead = rows[:, None] == partner[None, :]
    moved = jnp.sum(
        jnp.where(to_partner, partner[None, :], 0) + jnp.where(to_lead, lead[None, :], 0), axis=1
    )
    return jnp.where(jnp.any(to_partner | to_lead, axis=1), moved, rows)


def plan(swaps, tile, row_groups, dtype=jnp.float32):
    width = tile // row_groups
    count = swaps.shape[2]
    partner = swaps[:, 1, :].reshape(-1)
    top = jnp.arange(2 * tile, dtype=jnp.int32)
    rows = jnp.concatenate([top, partner])
    source = swapped(swapped(rows, swaps[1, 0], swaps[1, 1]), swaps[0, 0], swaps[0, 1])
    repeated = jnp.any(swaps[0, 1][:, None] == swaps[1, 1][None, :], axis=1)
    valid = jnp.concatenate([~repeated, jnp.ones((count,), bool)]) & (partner >= 2 * tile)
    sliced = source.reshape(3, row_groups, width).transpose(1, 0, 2)
    return rows, source, sliced, jnp.where(valid, partner, -1)


def hits(rows, first, tile):
    return (rows[:, None] == first + jnp.arange(tile, dtype=jnp.int32)[None, :]).astype(jnp.float32)


MESH = pl.DeviceIdType.MESH


def remote(src, dst, send, recv, device):
    return pltpu.make_async_remote_copy(
        src_ref=src, dst_ref=dst, send_sem=send, recv_sem=recv, device_id=device, device_id_type=MESH
    )


def exchange_kernel(
    sizes,
    picked,
    moves,
    strip,
    wide,
    corner,
    special,
    arrived,
    shares,
    share,
    share_in,
    cross,
    summed,
    rs_send,
    rs_recv,
    ag_send,
    ag_recv,
    z_send,
    z_recv,
    x_send,
    x_recv,
    f_send,
    f_recv,
    cz_send,
    cz_recv,
    cx_send,
    cx_recv,
    cg_send,
    cg_recv,
    cr_send,
    cr_recv,
    sp_send,
    sp_recv,
):
    rows_n, x_n, z_n, width = sizes
    r = lax.axis_index("row")
    x = lax.axis_index("col_0")
    z = lax.axis_index("col_1")

    def row_peer(d):
        return (lax.rem(r + d, rows_n), x, z)

    def z_peer(d):
        return (r, x, lax.rem(z + d + z_n, z_n))

    def x_peer(d):
        return (r, lax.rem(x + d + x_n, x_n), z)

    barrier = pltpu.get_barrier_semaphore()
    for d in range(1, rows_n):
        pl.semaphore_signal(barrier, inc=1, device_id=row_peer(d), device_id_type=MESH)
    for d in range(1, z_n):
        pl.semaphore_signal(barrier, inc=1, device_id=z_peer(d), device_id_type=MESH)
    for d in range(1, x_n):
        pl.semaphore_signal(barrier, inc=1, device_id=x_peer(d), device_id_type=MESH)
    pl.semaphore_wait(barrier, rows_n + z_n + x_n - 3)

    def reduce_copy(d):
        return remote(
            picked.at[lax.rem(r + d, rows_n)],
            arrived.at[d - 1],
            rs_send.at[d - 1],
            rs_recv.at[d - 1],
            row_peer(d),
        )

    for d in range(1, rows_n):
        reduce_copy(d).start()
    total = picked[r]
    for d in range(1, rows_n):
        reduce_copy(d).wait_recv()
        total = total + arrived[d - 1]
    strip[r] = total

    def gather_copy(d):
        return remote(
            strip.at[r], strip.at[r], ag_send.at[d - 1], ag_recv.at[d - 1], row_peer(d)
        )

    def gathered(d):
        q = lax.rem(r - d + rows_n, rows_n)
        return remote(
            strip.at[q], strip.at[q], ag_send.at[d - 1], ag_recv.at[d - 1], row_peer(d)
        )

    for d in range(1, rows_n):
        gather_copy(d).start()

    offset = lax.rem(z - r + z_n, z_n)
    half = z_n // 2
    is_root = offset == 0
    upward = offset <= half
    passes = ((offset > 0) & (offset < half)) | (offset > half + 1)
    ahead = jnp.where(upward, 1, z_n - 1)

    def z_copy(src, q, d, slot, step):
        return remote(
            src, wide.at[x, q], z_send.at[slot, d], z_recv.at[d], z_peer(step)
        )

    def x_copy(src, q, d, side):
        return remote(
            src,
            wide.at[x, q],
            x_send.at[side, d],
            x_recv.at[side, d],
            x_peer(1 if side == 0 else x_n - 1),
        )

    def f_copy(d, q):
        if d % 2 == 0:
            held = wide.at[lax.rem(x + x_n - 1, x_n), q]
            return remote(held, held, f_send.at[d], f_recv.at[d], x_peer(1))
        held = wide.at[lax.rem(x + 1, x_n), q]
        return remote(held, held, f_send.at[d], f_recv.at[d], x_peer(x_n - 1))

    def own_piece(d):
        q = lax.rem(r - d + rows_n, rows_n)

        @pl.when(is_root)
        def _():
            if d > 0:
                gathered(d).wait_recv()
            z_copy(strip.at[q], q, d, 0, 1).start()
            z_copy(strip.at[q], q, d, 1, z_n - 1).start()
            x_copy(strip.at[q], q, d, 0).start()
            x_copy(strip.at[q], q, d, 1).start()
            wide[x, q] = strip[q]

        @pl.when(jnp.logical_not(is_root))
        def _():
            z_copy(wide.at[x, q], q, d, 0, ahead).wait_recv()

            @pl.when(passes)
            def _():
                z_copy(wide.at[x, q], q, d, 0, ahead).start()

            x_copy(wide.at[x, q], q, d, 0).start()
            x_copy(wide.at[x, q], q, d, 1).start()

    def side_piece(d):
        q = lax.rem(r - d + rows_n, rows_n)
        x_copy(wide.at[x, q], q, d, 0).wait_recv()
        if d % 2 == 0:
            f_copy(d, q).start()
        x_copy(wide.at[x, q], q, d, 1).wait_recv()
        if d % 2 == 1:
            f_copy(d, q).start()

    def share_copy(d):
        return remote(
            shares.at[lax.rem(z + d, z_n)],
            share_in.at[d - 1],
            cz_send.at[d - 1],
            cz_recv.at[d - 1],
            z_peer(d),
        )

    def cross_copy(d):
        return remote(share, cross.at[d - 1], cx_send.at[d - 1], cx_recv.at[d - 1], x_peer(d))

    def share_back(d):
        return remote(
            summed.at[z], summed.at[z], cg_send.at[d - 1], cg_recv.at[d - 1], z_peer(d)
        )

    def share_taken(d):
        q = lax.rem(z - d + z_n, z_n)
        return remote(
            summed.at[q], summed.at[q], cg_send.at[d - 1], cg_recv.at[d - 1], z_peer(d)
        )

    own_piece(0)

    part = jnp.dot(
        strip[r], moves[...], precision=HI, preferred_element_type=jnp.float32
    )
    tile = moves.shape[1] // 3
    blocks = (
        (0, 2), (1, 2), (2, 2), (0, 1), (0, 0), (1, 1)
    )
    stacked = jnp.concatenate(
        [
            part[i * width : (i + 1) * width, j * tile : (j + 1) * tile]
            for i, j in blocks
        ],
        axis=0,
    )
    depth = 6 * width // z_n
    for n in range(z_n):
        shares[n] = stacked[n * depth : (n + 1) * depth]
    for d in range(1, z_n):
        share_copy(d).start()

    own_piece(1)
    side_piece(0)
    own_piece(2)
    side_piece(1)

    value = shares[z]
    for d in range(1, z_n):
        share_copy(d).wait_recv()
        value = value + share_in[d - 1]
    share[...] = value
    for d in range(1, x_n):
        cross_copy(d).start()

    if rows_n > 4:
        own_piece(3)
        side_piece(2)
    for d in range(1, x_n):
        cross_copy(d).wait_recv()
        value = value + cross[d - 1]
    summed[z] = value
    for d in range(1, z_n):
        share_back(d).start()

    first = 4 if rows_n > 4 else 3
    for d in range(first, rows_n):
        own_piece(d)
        side_piece(d - 1)
        if d == rows_n - 2 or rows_n == 4:
            for e in range(1, z_n):
                share_taken(e).wait_recv()
            flat = jnp.concatenate([summed[n] for n in range(z_n)], axis=0)
            corner[r] = flat[: 4 * width]
            special[r] = flat[4 * width :]
            for e in range(1, rows_n):
                remote(
                    corner.at[r], corner.at[r], cr_send.at[e - 1], cr_recv.at[e - 1], row_peer(e)
                ).start()
            for home in range(2):
                @pl.when((x == 0) & (z == home) & (r != home))
                def _():
                    remote(
                        special.at[r],
                        special.at[r],
                        sp_send,
                        sp_recv.at[r],
                        (home, x, z),
                    ).start()
    side_piece(rows_n - 1)

    for d in range(1, rows_n):
        @pl.when(jnp.logical_not(is_root))
        def _():
            gathered(d).wait_recv()

        q = lax.rem(r - d + rows_n, rows_n)
        remote(
            corner.at[q], corner.at[q], cr_send.at[d - 1], cr_recv.at[d - 1], row_peer(d)
        ).wait()
        reduce_copy(d).wait_send()
        gather_copy(d).wait_send()
    for d in range(rows_n):
        q = lax.rem(r - d + rows_n, rows_n)
        f_copy(d, q).wait()
        x_copy(wide.at[x, q], q, d, 0).wait_send()
        x_copy(wide.at[x, q], q, d, 1).wait_send()

        @pl.when(is_root | passes)
        def _():
            z_copy(wide.at[x, q], q, d, 0, ahead).wait_send()

        @pl.when(is_root)
        def _():
            z_copy(wide.at[x, q], q, d, 1, ahead).wait_send()

    for d in range(1, z_n):
        share_copy(d).wait_send()
        share_back(d).wait_send()
    for d in range(1, x_n):
        cross_copy(d).wait_send()
    for home in range(2):
        for n in range(rows_n):
            if n != home:
                here = (x == 0) & (z == home)

                @pl.when(here & (r == n))
                def _():
                    remote(
                        special.at[n], special.at[n], sp_send, sp_recv.at[n], (home, x, z)
                    ).wait_send()

                @pl.when(here & (r == home))
                def _():
                    remote(
                        special.at[n], special.at[n], sp_send, sp_recv.at[n], (n, x, z)
                    ).wait_recv()


def exchange(picked, moves, tile, rows_n, x_n):
    z_n = rows_n
    width = tile // rows_n
    depth = 6 * width // z_n
    f32 = jnp.float32
    dma = pltpu.SemaphoreType.DMA
    vmem = pl.BlockSpec(memory_space=pltpu.VMEM)
    return pl.pallas_call(
        functools.partial(exchange_kernel, (rows_n, x_n, z_n, width)),
        out_shape=(
            jax.ShapeDtypeStruct((rows_n, 3 * width, tile), f32),
            jax.ShapeDtypeStruct((x_n, rows_n, 3 * width, tile), f32),
            jax.ShapeDtypeStruct((rows_n, 4 * width, tile), f32),
            jax.ShapeDtypeStruct((rows_n, 2 * width, tile), f32),
        ),
        in_specs=[vmem] * 2,
        out_specs=(vmem,) * 4,
        scratch_shapes=[
            pltpu.VMEM((rows_n - 1, 3 * width, tile), f32),
            pltpu.VMEM((z_n, depth, tile), f32),
            pltpu.VMEM((depth, tile), f32),
            pltpu.VMEM((z_n - 1, depth, tile), f32),
            pltpu.VMEM((x_n - 1, depth, tile), f32),
            pltpu.VMEM((z_n, depth, tile), f32),
            dma((rows_n - 1,)),
            dma((rows_n - 1,)),
            dma((rows_n - 1,)),
            dma((rows_n - 1,)),
            dma((2, rows_n)),
            dma((rows_n,)),
            dma((2, rows_n)),
            dma((2, rows_n)),
            dma((rows_n,)),
            dma((rows_n,)),
            dma((z_n - 1,)),
            dma((z_n - 1,)),
            dma((x_n - 1,)),
            dma((x_n - 1,)),
            dma((z_n - 1,)),
            dma((z_n - 1,)),
            dma((rows_n - 1,)),
            dma((rows_n - 1,)),
            dma,
            dma((rows_n,)),
        ],
        compiler_params=pltpu.CompilerParams(collective_id=0, has_side_effects=True),
    )(picked, moves)


BF = jnp.bfloat16


def halves(a):
    high = a.astype(BF)
    return high, (a - high.astype(jnp.float32)).astype(BF)


def dot_n(a, b, dims):
    return lax.dot_general(a, b, (dims, ((), ())), preferred_element_type=jnp.float32)


def dot3(a, b, dims):
    return dot_n(a[0], b[0], dims) + (dot_n(a[0], b[1], dims) + dot_n(a[1], b[0], dims))


NN = ((1,), (0,))
TN = ((0,), (0,))


def update_kernel(
    kkt,
    wide,
    strip,
    corner,
    special,
    inverses,
    pivots,
    couplings,
    pattern,
    partner_col,
    partner_row,
    out,
    coef,
):
    x_n, rows_n, deep, tile = wide.shape
    width = deep // 3
    r = lax.axis_index("row")
    c = lax.axis_index("col_0") * lax.axis_size("col_1") + lax.axis_index("col_1")
    lanes = lax.broadcasted_iota(jnp.int32, (2, tile), 1)
    links = couplings[...] * pattern[...].astype(jnp.float32)
    links = jnp.where(lanes == tile - 1, 0.0, links)
    coef[...] = jnp.zeros_like(coef)
    coef[0:2, :] = pivots[...]
    coef[2:4, :] = links
    coef[4:6, :] = jnp.where(lanes == 0, 0.0, pltpu.roll(links, 1, 1))
    table = coef[...].T

    def along_d(lower_t, panel):
        pivot = table[:, panel : panel + 1]
        after = table[:, 2 + panel : 3 + panel]
        before = table[:, 4 + panel : 5 + panel]
        return (
            lower_t * pivot
            + pltpu.roll(lower_t, tile - 1, 0) * after
            + pltpu.roll(lower_t, 1, 0) * before
        )

    def rows_of(ref, part):
        return jnp.concatenate(
            [ref[q, part * width : (part + 1) * width, :] for q in range(rows_n)], axis=0
        )

    tiles = [r + rows_n * slot for slot in range(x_n)] + [c]
    inv0 = halves(inverses[0].T)
    inv1 = halves(inverses[1].T)
    block_01 = rows_of(corner, 3)
    low0_1 = dot3(inv0, halves(block_01), NN)
    scaled0_1 = along_d(low0_1, 0)
    scaled0_1_rows = halves(scaled0_1.T)
    to_partner = [halves(rows_of(corner, part)) for part in range(3)]
    columns = lax.broadcasted_iota(jnp.int32, (tile, tile), 1)
    depths = lax.broadcasted_iota(jnp.int32, (tile, tile), 0)

    def panels(n):
        ref = strip if n == x_n else wide.at[n]
        index = tiles[n]
        hit = (partner_col[...] - index * tile) == columns
        mark = jnp.where(hit, 1.0, 0.0).astype(BF)
        keep = 1.0 - jnp.sum(jnp.where(hit, 1.0, 0.0), axis=0, keepdims=True)
        fixed = [
            rows_of(ref, part) * keep
            + dot_n(to_partner[part][0], mark, NN)
            + dot_n(to_partner[part][1], mark, NN)
            for part in range(3)
        ]
        upper = jnp.where(index == 1, block_01, fixed[0])
        low0 = dot3(inv0, halves(upper), NN) * jnp.where(index > 0, 1.0, 0.0)
        below = fixed[1] - dot3(scaled0_1_rows, halves(low0), NN)
        low1 = dot3(inv1, halves(below), NN) * jnp.where(index > 1, 1.0, 0.0)
        return low0, low1, fixed[2], mark, keep

    low0_c, low1_c, moved_c, mark_c, keep_c = panels(x_n)
    scaled0 = along_d(low0_c, 0)
    scaled1 = along_d(low1_c, 1)
    scaled0_h = halves(scaled0)
    scaled1_h = halves(scaled1)
    moved_h = halves(moved_c)

    for n in range(x_n):
        low0, low1, moved, mark, keep = panels(n)
        place = slice(n * tile, (n + 1) * tile)

        @pl.when(c > 1)
        def _():
            hit = (partner_row[...] - tiles[n] * tile) == depths
            keep_rows = 1.0 - jnp.sum(jnp.where(hit, 1.0, 0.0), axis=1, keepdims=True)
            value = kkt[place, :] * keep_rows * keep_c
            value = value + dot_n(mark, moved_h[0], TN) + dot_n(mark, moved_h[1], TN)
            across = halves(moved * keep)
            value = value + dot_n(across[0], mark_c, TN) + dot_n(across[1], mark_c, TN)
            value = value - dot3(halves(low0), scaled0_h, TN)
            value = value - dot3(halves(low1), scaled1_h, TN)
            if n == 0:
                value = jnp.where(r == 0, scaled0, jnp.where(r == 1, scaled1, value))
            out[place, :] = value

        @pl.when(c == 0)
        def _():
            value = low0.T
            if n == 0:
                value = jnp.where(r == 0, rows_of(special, 0), value)
            out[place, :] = value

        @pl.when(c == 1)
        def _():
            value = low1.T
            if n == 0:
                first = rows_of(special, 1) - dot3(halves(low0_1), halves(scaled0_1), TN)
                value = jnp.where(r == 0, scaled0_1, jnp.where(r == 1, first, value))
            out[place, :] = value


def update(kkt, wide, strip, corner, special, inverses, pivots, couplings, pattern, partner):
    tile = kkt.shape[1]
    vmem = pl.BlockSpec(memory_space=pltpu.VMEM)
    return pl.pallas_call(
        update_kernel,
        out_shape=jax.ShapeDtypeStruct(kkt.shape, jnp.float32),
        in_specs=[vmem] * 11,
        out_specs=vmem,
        scratch_shapes=[pltpu.VMEM((128, tile), jnp.float32)],
    )(
        kkt,
        wide,
        strip,
        corner,
        special,
        inverses,
        pivots,
        couplings,
        pattern,
        partner[:, None],
        partner[None, :],
    )


def shards(kkt, swaps, inverses, pivots, couplings, pattern):
    tile = inverses.shape[1]
    row_groups = lax.axis_size("row")
    x_size = lax.axis_size("col_0")
    z_size = lax.axis_size("col_1")
    row_index = lax.axis_index("row")
    col_index = lax.axis_index(COL)
    rows, source, sliced, partner = plan(swaps, tile, row_groups)
    flat = sliced.reshape(-1)
    owned = flat // tile % row_groups == row_index
    taken = jnp.take(kkt, flat // tile // row_groups * tile + flat % tile, axis=0)
    picked = jnp.where(owned[:, None], taken, 0.0).reshape(row_groups, -1, tile)
    moves = hits(source, col_index * tile, tile).T
    strip, wide, corner, special = exchange(picked, moves, tile, row_groups, x_size)

    return update(
        kkt, wide, strip, corner, special, inverses, pivots, couplings, pattern, partner
    )


def solution(mesh):
    z_size = mesh.shape["row"]
    finer = Mesh(mesh.devices.reshape(mesh.shape["row"], -1, z_size), ("row", "col_0", "col_1"))
    in_specs = (P("row", COL), P(), P(), P(), P(), P())
    return jax.shard_map(
        shards, mesh=finer, in_specs=in_specs, out_specs=P("row", COL), check_vma=False
    )
```

```python
import functools

import jax
import jax.numpy as jnp
from jax import lax
from jax.experimental import pallas as pl
from jax.experimental.pallas import tpu as pltpu
from jax.sharding import Mesh
from jax.sharding import PartitionSpec as P

COL = ("col_0", "col_1")
HI = lax.Precision.HIGHEST


def swapped(rows, lead, partner):
    to_partner = rows[:, None] == lead[None, :]
    to_lead = rows[:, None] == partner[None, :]
    moved = jnp.sum(
        jnp.where(to_partner, partner[None, :], 0) + jnp.where(to_lead, lead[None, :], 0), axis=1
    )
    return jnp.where(jnp.any(to_partner | to_lead, axis=1), moved, rows)


def plan(swaps, tile, row_groups, dtype=jnp.float32):
    width = tile // row_groups
    count = swaps.shape[2]
    partner = swaps[:, 1, :].reshape(-1)
    top = jnp.arange(2 * tile, dtype=jnp.int32)
    rows = jnp.concatenate([top, partner])
    source = swapped(swapped(rows, swaps[1, 0], swaps[1, 1]), swaps[0, 0], swaps[0, 1])
    repeated = jnp.any(swaps[0, 1][:, None] == swaps[1, 1][None, :], axis=1)
    valid = jnp.concatenate([~repeated, jnp.ones((count,), bool)]) & (partner >= 2 * tile)
    sliced = source.reshape(3, row_groups // 2, 2, width).transpose(2, 1, 0, 3)
    return rows, source, sliced, jnp.where(valid, partner, -1)


def hits(rows, first, tile):
    return (rows[:, None] == first + jnp.arange(tile, dtype=jnp.int32)[None, :]).astype(jnp.float32)


MESH = pl.DeviceIdType.MESH


def remote(src, dst, send, recv, device):
    return pltpu.make_async_remote_copy(
        src_ref=src, dst_ref=dst, send_sem=send, recv_sem=recv, device_id=device, device_id_type=MESH
    )


def exchange_kernel(
    sizes,
    picked,
    moves,
    strip,
    wide,
    corner,
    special,
    near_in,
    chip_sum,
    far_in,
    shares,
    share,
    share_in,
    cross,
    summed,
    p_send,
    p_recv,
    r_send,
    r_recv,
    g_send,
    g_recv,
    h_send,
    h_recv,
    z_send,
    z_recv,
    x_send,
    x_recv,
    f_send,
    f_recv,
    cz_send,
    cz_recv,
    cx_send,
    cx_recv,
    cg_send,
    cg_recv,
    cr_send,
    cr_recv,
    ch_send,
    ch_recv,
    sp_send,
    sp_recv,
):
    y_n, x_n, z_n, width = sizes
    rows_n = 2 * y_n
    r = lax.axis_index("row")
    x = lax.axis_index("col_0")
    z = lax.axis_index("col_1")
    y = r // 2
    k = lax.rem(r, 2)
    twin = (r + 1 - 2 * k, x, z)

    def y_peer(d):
        return (lax.rem(r + 2 * d, rows_n), x, z)

    def z_peer(d):
        return (r, x, lax.rem(z + d + z_n, z_n))

    def x_peer(d):
        return (r, lax.rem(x + d + x_n, x_n), z)

    def owner(d, flip):
        core = k if flip == 0 else 1 - k
        return 2 * lax.rem(y - d + y_n, y_n) + core

    barrier = pltpu.get_barrier_semaphore()
    pl.semaphore_signal(barrier, inc=1, device_id=twin, device_id_type=MESH)
    for d in range(1, y_n):
        pl.semaphore_signal(barrier, inc=1, device_id=y_peer(d), device_id_type=MESH)
    for d in range(1, z_n):
        pl.semaphore_signal(barrier, inc=1, device_id=z_peer(d), device_id_type=MESH)
    for d in range(1, x_n):
        pl.semaphore_signal(barrier, inc=1, device_id=x_peer(d), device_id_type=MESH)
    for d in range(1, y_n):
        there = (2 * lax.rem(y + d, y_n) + 1 - k, x, z)
        pl.semaphore_signal(barrier, inc=1, device_id=there, device_id_type=MESH)
    pl.semaphore_wait(barrier, 2 * y_n + z_n + x_n - 3)

    def chip_copy(d):
        n = lax.rem(y + d, y_n)
        return remote(picked.at[1 - k, n], near_in.at[d], p_send.at[d], p_recv.at[d], twin)

    def y_copy(d):
        return remote(
            chip_sum.at[d - 1], far_in.at[d - 1], r_send.at[d - 1], r_recv.at[d - 1], y_peer(d)
        )

    order = [2, 1, 3, 0] if y_n == 4 else list(range(1, y_n)) + [0]
    for d in order:
        chip_copy(d).start()
    for d in order[:-1]:
        chip_copy(d).wait_recv()
        chip_sum[d - 1] = picked[k, lax.rem(y + d, y_n)] + near_in[d]
        y_copy(d).start()
    chip_copy(0).wait_recv()
    total = picked[k, y] + near_in[0]
    for d in range(1, y_n):
        y_copy(d).wait_recv()
        total = total + far_in[d - 1]
    strip[r] = total

    def gather_copy(ref, d, send, recv):
        return remote(ref.at[r], ref.at[r], send.at[d - 1], recv.at[d - 1], y_peer(d))

    def gathered(ref, d, send, recv):
        q = owner(d, 0)
        return remote(ref.at[q], ref.at[q], send.at[d - 1], recv.at[d - 1], y_peer(d))

    def twin_copy(ref, d, flip, send, recv):
        q = owner(d, flip)
        return remote(ref.at[q], ref.at[q], send.at[d], recv.at[d], twin)

    for d in range(1, y_n):
        gather_copy(strip, d, g_send, g_recv).start()
    twin_copy(strip, 0, 0, h_send, h_recv).start()

    offset = lax.rem(z - r + z_n, z_n)
    half = z_n // 2
    is_root = offset == 0
    not_root = jnp.logical_not(is_root)
    upward = offset <= half
    passes = ((offset > 0) & (offset < half)) | (offset > half + 1)
    ahead = jnp.where(upward, 1, z_n - 1)
    reach = jnp.minimum(offset, z_n - offset)
    is_near = reach <= 1
    is_mid = reach == 2
    is_far = reach > 2
    cut = 3 * width // 2
    if y_n == 4:
        turn = [(0, 0), (0, 1), (1, 0), (3, 0), (1, 1), (3, 1), (2, 0), (2, 1)]
    else:
        turn = [(d, flip) for d in range(y_n) for flip in range(2)]
    pieces = 2 * rows_n

    def spot(i):
        q = owner(*turn[i // 2])
        return q, pl.ds((i % 2) * cut, cut)

    def z_copy(src, i, slot, step):
        q, part = spot(i)
        return remote(
            src.at[q, part], wide.at[x, q, part], z_send.at[slot, i], z_recv.at[i], z_peer(step)
        )

    def x_copy(src, i, side):
        q, part = spot(i)
        return remote(
            src.at[q, part],
            wide.at[x, q, part],
            x_send.at[side, i],
            x_recv.at[side, i],
            x_peer(1 if side == 0 else x_n - 1),
        )

    def f_copy(i):
        q, part = spot(i)
        step = 1 if i % 2 == 0 else x_n - 1
        held = wide.at[lax.rem(x + x_n - step, x_n), q, part]
        return remote(held, held, f_send.at[i], f_recv.at[i], x_peer(step))

    def own_piece(i):
        q, part = spot(i)
        d, flip = turn[i // 2]

        @pl.when(is_root)
        def _():
            if i % 2 == 0 and flip == 1:
                twin_copy(strip, d, 1, h_send, h_recv).wait_recv()
            z_copy(strip, i, 0, 1).start()
            z_copy(strip, i, 1, z_n - 1).start()
            x_copy(strip, i, 0).start()
            x_copy(strip, i, 1).start()
            wide[x, q, part] = strip[q, part]

        @pl.when(not_root)
        def _():
            z_copy(wide.at[x], i, 0, ahead).wait_recv()

            @pl.when(passes)
            def _():
                z_copy(wide.at[x], i, 0, ahead).start()

            x_copy(wide.at[x], i, 0).start()
            x_copy(wide.at[x], i, 1).start()

    def side_piece(i):
        for side in (i % 2, 1 - i % 2):
            x_copy(wide.at[x], i, side).wait_recv()
            if side == i % 2:
                f_copy(i).start()

    def share_copy(d):
        return remote(
            shares.at[lax.rem(z + d, z_n)],
            share_in.at[d - 1],
            cz_send.at[d - 1],
            cz_recv.at[d - 1],
            z_peer(d),
        )

    def cross_copy(d):
        return remote(share, cross.at[d - 1], cx_send.at[d - 1], cx_recv.at[d - 1], x_peer(d))

    def share_back(d):
        return remote(
            summed.at[z], summed.at[z], cg_send.at[d - 1], cg_recv.at[d - 1], z_peer(d)
        )

    def share_taken(d):
        q = lax.rem(z - d + z_n, z_n)
        return remote(
            summed.at[q], summed.at[q], cg_send.at[d - 1], cg_recv.at[d - 1], z_peer(d)
        )

    def corner_z():
        value = shares[z]
        for d in range(1, z_n):
            share_copy(d).wait_recv()
            value = value + share_in[d - 1]
        share[...] = value
        for d in range(1, x_n):
            cross_copy(d).start()

    def corner_x():
        value = share[...]
        for d in range(1, x_n):
            cross_copy(d).wait_recv()
            value = value + cross[d - 1]
        summed[z] = value
        for d in range(1, z_n):
            share_back(d).start()

    def corner_back():
        for d in range(1, z_n):
            share_taken(d).wait_recv()
        flat = jnp.concatenate([summed[n] for n in range(z_n)], axis=0)
        corner[r] = flat[: 4 * width]
        special[r] = flat[4 * width :]
        for d in range(1, y_n):
            gather_copy(corner, d, cr_send, cr_recv).start()
        twin_copy(corner, 0, 0, ch_send, ch_recv).start()
        for home in range(2):
            @pl.when((x == 0) & (z == home) & (r != home))
            def _():
                remote(
                    special.at[r], special.at[r], sp_send, sp_recv.at[r], (home, x, z)
                ).start()

    def corner_twin():
        for d in range(1, y_n):
            gathered(corner, d, cr_send, cr_recv).wait_recv()
            twin_copy(corner, d, 0, ch_send, ch_recv).start()

    steps = [corner_z, corner_x, corner_back, corner_twin]
    spots = {True: [[3, 5, 11, 14], [1, 3, 9, 13], [-1, -1, 6, 11]], False: [[2, 3, 5, 6]] * 3}
    spots = spots[pieces == 16]

    def corner_steps(i):
        for kind, at in zip((is_near, is_mid, is_far), spots):
            if i in at:

                @pl.when(kind)
                def _():
                    for step, place in zip(steps, at):
                        if place == i:
                            step()

    @pl.when(is_root)
    def _():
        for i in range(2):
            q, part = spot(i)
            z_copy(strip, i, 0, 1).start()
            z_copy(strip, i, 1, z_n - 1).start()
            x_copy(strip, i, 0).start()
            x_copy(strip, i, 1).start()
            wide[x, q, part] = strip[q, part]

    part = jnp.dot(strip[r], moves[...], precision=HI, preferred_element_type=jnp.float32)
    tile = moves.shape[1] // 3
    blocks = ((0, 2), (1, 2), (2, 2), (0, 1), (0, 0), (1, 1))
    stacked = jnp.concatenate(
        [
            part[i * width : (i + 1) * width, j * tile : (j + 1) * tile]
            for i, j in blocks
        ],
        axis=0,
    )
    depth = 6 * width // z_n
    for n in range(z_n):
        shares[n] = stacked[n * depth : (n + 1) * depth]
    for d in range(1, z_n):
        share_copy(d).start()

    for d in (1, 3, 2) if y_n == 4 else range(1, y_n):
        gathered(strip, d, g_send, g_recv).wait_recv()
        twin_copy(strip, d, 0, h_send, h_recv).start()

    corner_steps(-1)
    lag = 2
    for i in range(pieces):
        if i > 1:
            own_piece(i)
        else:

            @pl.when(not_root)
            def _():
                z_copy(wide.at[x], i, 0, ahead).wait_recv()

                @pl.when(passes)
                def _():
                    z_copy(wide.at[x], i, 0, ahead).start()

                x_copy(wide.at[x], i, 0).start()
                x_copy(wide.at[x], i, 1).start()

        corner_steps(i)
        if i >= lag:
            side_piece(i - lag)
    for i in range(pieces - lag, pieces):
        side_piece(i)

    for d in range(y_n):
        @pl.when(not_root)
        def _():
            twin_copy(strip, d, 1, h_send, h_recv).wait_recv()

        twin_copy(strip, d, 0, h_send, h_recv).wait_send()
        twin_copy(corner, d, 1, ch_send, ch_recv).wait_recv()
        twin_copy(corner, d, 0, ch_send, ch_recv).wait_send()
        chip_copy(d).wait_send()
    for d in range(1, y_n):
        y_copy(d).wait_send()
        gather_copy(strip, d, g_send, g_recv).wait_send()
        gather_copy(corner, d, cr_send, cr_recv).wait_send()
    for i in range(pieces):
        f_copy(i).wait()
        x_copy(wide.at[x], i, 0).wait_send()
        x_copy(wide.at[x], i, 1).wait_send()

        @pl.when(is_root | passes)
        def _():
            z_copy(wide.at[x], i, 0, ahead).wait_send()

        @pl.when(is_root)
        def _():
            z_copy(wide.at[x], i, 1, ahead).wait_send()

    for d in range(1, z_n):
        share_copy(d).wait_send()
        share_back(d).wait_send()
    for d in range(1, x_n):
        cross_copy(d).wait_send()
    for home in range(2):
        for n in range(rows_n):
            if n != home:
                here = (x == 0) & (z == home)

                @pl.when(here & (r == n))
                def _():
                    remote(
                        special.at[n], special.at[n], sp_send, sp_recv.at[n], (home, x, z)
                    ).wait_send()

                @pl.when(here & (r == home))
                def _():
                    remote(
                        special.at[n], special.at[n], sp_send, sp_recv.at[n], (n, x, z)
                    ).wait_recv()


def exchange(picked, moves, tile, rows_n, x_n):
    z_n = rows_n
    y_n = rows_n // 2
    width = tile // rows_n
    depth = 6 * width // z_n
    f32 = jnp.float32
    dma = pltpu.SemaphoreType.DMA
    vmem = pl.BlockSpec(memory_space=pltpu.VMEM)
    return pl.pallas_call(
        functools.partial(exchange_kernel, (y_n, x_n, z_n, width)),
        out_shape=(
            jax.ShapeDtypeStruct((rows_n, 3 * width, tile), f32),
            jax.ShapeDtypeStruct((x_n, rows_n, 3 * width, tile), f32),
            jax.ShapeDtypeStruct((rows_n, 4 * width, tile), f32),
            jax.ShapeDtypeStruct((rows_n, 2 * width, tile), f32),
        ),
        in_specs=[vmem] * 2,
        out_specs=(vmem,) * 4,
        scratch_shapes=[
            pltpu.VMEM((y_n, 3 * width, tile), f32),
            pltpu.VMEM((y_n - 1, 3 * width, tile), f32),
            pltpu.VMEM((y_n - 1, 3 * width, tile), f32),
            pltpu.VMEM((z_n, depth, tile), f32),
            pltpu.VMEM((depth, tile), f32),
            pltpu.VMEM((z_n - 1, depth, tile), f32),
            pltpu.VMEM((x_n - 1, depth, tile), f32),
            pltpu.VMEM((z_n, depth, tile), f32),
            dma((y_n,)),
            dma((y_n,)),
            dma((y_n - 1,)),
            dma((y_n - 1,)),
            dma((y_n - 1,)),
            dma((y_n - 1,)),
            dma((y_n,)),
            dma((y_n,)),
            dma((2, 2 * rows_n)),
            dma((2 * rows_n,)),
            dma((2, 2 * rows_n)),
            dma((2, 2 * rows_n)),
            dma((2 * rows_n,)),
            dma((2 * rows_n,)),
            dma((z_n - 1,)),
            dma((z_n - 1,)),
            dma((x_n - 1,)),
            dma((x_n - 1,)),
            dma((z_n - 1,)),
            dma((z_n - 1,)),
            dma((y_n - 1,)),
            dma((y_n - 1,)),
            dma((y_n,)),
            dma((y_n,)),
            dma,
            dma((rows_n,)),
        ],
        compiler_params=pltpu.CompilerParams(collective_id=0, has_side_effects=True),
    )(picked, moves)


BF = jnp.bfloat16


def halves(a):
    high = a.astype(BF)
    return high, (a - high.astype(jnp.float32)).astype(BF)


def dot_n(a, b, dims):
    return lax.dot_general(a, b, (dims, ((), ())), preferred_element_type=jnp.float32)


def dot3(a, b, dims):
    return dot_n(a[0], b[0], dims) + (dot_n(a[0], b[1], dims) + dot_n(a[1], b[0], dims))


NN = ((1,), (0,))


def update_kernel(
    kkt,
    wide,
    strip,
    corner,
    special,
    inverses,
    pivots,
    couplings,
    pattern,
    partner_col,
    partner_row,
    out,
    coef,
):
    x_n, rows_n, deep, tile = wide.shape
    width = deep // 3
    r = lax.axis_index("row")
    c = lax.axis_index("col_0") * lax.axis_size("col_1") + lax.axis_index("col_1")
    lanes = lax.broadcasted_iota(jnp.int32, (2, tile), 1)
    links = couplings[...] * pattern[...].astype(jnp.float32)
    links = jnp.where(lanes == tile - 1, 0.0, links)
    coef[...] = jnp.zeros_like(coef)
    coef[0:2, :] = pivots[...]
    coef[2:4, :] = links
    coef[4:6, :] = jnp.where(lanes == 0, 0.0, pltpu.roll(links, 1, 1))
    table = coef[...].T

    def along_d(lower_t, panel):
        pivot = table[:, panel : panel + 1]
        after = table[:, 2 + panel : 3 + panel]
        before = table[:, 4 + panel : 5 + panel]
        return (
            lower_t * pivot
            + pltpu.roll(lower_t, tile - 1, 0) * after
            + pltpu.roll(lower_t, 1, 0) * before
        )

    def rows_of(ref, part):
        return jnp.concatenate(
            [ref[q, part * width : (part + 1) * width, :] for q in range(rows_n)], axis=0
        )

    tiles = [r + rows_n * slot for slot in range(x_n)] + [c]
    inv0 = halves(inverses[0].T)
    inv1 = halves(inverses[1].T)
    block_01 = rows_of(corner, 3)
    low0_1 = dot3(inv0, halves(block_01), NN)
    scaled0_1 = along_d(low0_1, 0)
    scaled0_1_rows = halves(scaled0_1.T)
    to_partner = [halves(rows_of(corner, part)) for part in range(3)]
    columns = lax.broadcasted_iota(jnp.int32, (tile, tile), 1)
    depths = lax.broadcasted_iota(jnp.int32, (tile, tile), 0)

    def panels(n):
        ref = strip if n == x_n else wide.at[n]
        index = tiles[n]
        hit = (partner_col[...] - index * tile) == columns
        mark = jnp.where(hit, 1.0, 0.0).astype(BF)
        keep = 1.0 - jnp.sum(jnp.where(hit, 1.0, 0.0), axis=0, keepdims=True)
        fixed = [
            rows_of(ref, part) * keep
            + dot_n(to_partner[part][0], mark, NN)
            + dot_n(to_partner[part][1], mark, NN)
            for part in range(3)
        ]
        upper = jnp.where(index == 1, block_01, fixed[0])
        low0 = dot3(inv0, halves(upper), NN) * jnp.where(index > 0, 1.0, 0.0)
        below = fixed[1] - dot3(scaled0_1_rows, halves(low0), NN)
        low1 = dot3(inv1, halves(below), NN) * jnp.where(index > 1, 1.0, 0.0)
        return low0, low1, fixed[2], mark, keep

    low0_c, low1_c, moved_c, mark_c, keep_c = panels(x_n)
    scaled0 = along_d(low0_c, 0)
    scaled1 = along_d(low1_c, 1)
    scaled0_rows = halves(scaled0.T)
    scaled1_rows = halves(scaled1.T)
    moved_rows = halves(moved_c.T)
    hit_c = (partner_row[...] - c * tile) == depths
    mark_rows = jnp.where(hit_c, 1.0, 0.0).astype(BF)

    for n in range(x_n):
        low0, low1, moved, mark, keep = panels(n)
        place = slice(n * tile, (n + 1) * tile)

        @pl.when(c > 1)
        def _():
            hit = (partner_row[...] - tiles[n] * tile) == depths
            keep_rows = 1.0 - jnp.sum(jnp.where(hit, 1.0, 0.0), axis=1, keepdims=True)
            across = halves(moved * keep)
            change = dot_n(moved_rows[0], mark, NN) + dot_n(moved_rows[1], mark, NN)
            change = change + dot_n(mark_rows, across[0], NN) + dot_n(mark_rows, across[1], NN)
            change = change - dot3(scaled0_rows, halves(low0), NN)
            change = change - dot3(scaled1_rows, halves(low1), NN)
            value = kkt[place, :] * keep_rows * keep_c + change.T
            if n == 0:
                value = jnp.where(r == 0, scaled0, jnp.where(r == 1, scaled1, value))
            out[place, :] = value

        @pl.when(c == 0)
        def _():
            value = low0.T
            if n == 0:
                value = jnp.where(r == 0, rows_of(special, 0), value)
            out[place, :] = value

        @pl.when(c == 1)
        def _():
            value = low1.T
            if n == 0:
                first = rows_of(special, 1) - dot3(scaled0_1_rows, halves(low0_1), NN).T
                value = jnp.where(r == 0, scaled0_1, jnp.where(r == 1, first, value))
            out[place, :] = value


def update(kkt, wide, strip, corner, special, inverses, pivots, couplings, pattern, partner):
    tile = kkt.shape[1]
    vmem = pl.BlockSpec(memory_space=pltpu.VMEM)
    return pl.pallas_call(
        update_kernel,
        out_shape=jax.ShapeDtypeStruct(kkt.shape, jnp.float32),
        in_specs=[vmem] * 11,
        out_specs=vmem,
        scratch_shapes=[pltpu.VMEM((128, tile), jnp.float32)],
    )(
        kkt,
        wide,
        strip,
        corner,
        special,
        inverses,
        pivots,
        couplings,
        pattern,
        partner[:, None],
        partner[None, :],
    )


def shards(kkt, swaps, inverses, pivots, couplings, pattern):
    tile = inverses.shape[1]
    row_groups = lax.axis_size("row")
    x_size = lax.axis_size("col_0")
    z_size = lax.axis_size("col_1")
    row_index = lax.axis_index("row")
    col_index = lax.axis_index(COL)
    rows, source, sliced, partner = plan(swaps, tile, row_groups)
    flat = sliced.reshape(-1)
    owned = flat // tile % row_groups == row_index
    taken = jnp.take(kkt, flat // tile // row_groups * tile + flat % tile, axis=0)
    picked = jnp.where(owned[:, None], taken, 0.0).reshape(2, row_groups // 2, -1, tile)
    moves = hits(source, col_index * tile, tile).T
    strip, wide, corner, special = exchange(picked, moves, tile, row_groups, x_size)

    return update(
        kkt, wide, strip, corner, special, inverses, pivots, couplings, pattern, partner
    )


def solution(mesh):
    z_size = mesh.shape["row"]
    finer = Mesh(mesh.devices.reshape(mesh.shape["row"], -1, z_size), ("row", "col_0", "col_1"))
    in_specs = (P("row", COL), P(), P(), P(), P(), P())
    return jax.shard_map(
        shards, mesh=finer, in_specs=in_specs, out_specs=P("row", COL), check_vma=False
    )
```

```python
import functools

import jax
import jax.numpy as jnp
from jax import lax
from jax.experimental import pallas as pl
from jax.experimental.pallas import tpu as pltpu
from jax.sharding import Mesh
from jax.sharding import PartitionSpec as P

COL = ("col_0", "col_1")
BF = jnp.bfloat16
F32 = jnp.float32
NN = ((1,), (0,))
NT = ((1,), (1,))


def halves(a):
    high = a.astype(BF)
    return high, (a - high.astype(F32)).astype(BF)


def dot_n(a, b, dims):
    return lax.dot_general(a, b, (dims, ((), ())), preferred_element_type=F32)


def dot3(a, b):
    return dot_n(a[0], b[0], NN) + (dot_n(a[0], b[1], NN) + dot_n(a[1], b[0], NN))


def swapped(rows, lead, partner):
    to_partner = rows == lead
    to_lead = rows == partner
    moved = jnp.where(to_partner, partner, 0.0) + jnp.where(to_lead, lead, 0.0)
    touched = jnp.where(to_partner | to_lead, 1.0, 0.0)
    moved = jnp.sum(moved, axis=1, keepdims=True)
    return jnp.where(jnp.sum(touched, axis=1, keepdims=True) > 0.0, moved, rows)


MESH = pl.DeviceIdType.MESH


def remote(src, dst, send, recv, device):
    return pltpu.make_async_remote_copy(
        src_ref=src, dst_ref=dst, send_sem=send, recv_sem=recv, device_id=device, device_id_type=MESH
    )


def step_kernel(
    sizes,
    kkt,
    swaps,
    inverses,
    pivots,
    couplings,
    pattern,
    out,
    coef,
    picked,
    strip,
    wide,
    corner,
    special,
    near_in,
    chip_sum,
    far_in,
    shares,
    share,
    share_in,
    cross,
    summed,
    p_send,
    p_recv,
    r_send,
    r_recv,
    g_send,
    g_recv,
    h_send,
    h_recv,
    z_send,
    z_recv,
    x_send,
    x_recv,
    f_send,
    f_recv,
    cz_send,
    cz_recv,
    cx_send,
    cx_recv,
    cg_send,
    cg_recv,
    cr_send,
    cr_recv,
    ch_send,
    ch_recv,
    sp_send,
    sp_recv,
):
    y_n, x_n, z_n, width = sizes
    rows_n = 2 * y_n
    r = lax.axis_index("row")
    x = lax.axis_index("col_0")
    z = lax.axis_index("col_1")
    y = r // 2
    k = lax.rem(r, 2)
    twin = (r + 1 - 2 * k, x, z)

    def y_peer(d):
        return (lax.rem(r + 2 * d, rows_n), x, z)

    def z_peer(d):
        return (r, x, lax.rem(z + d + z_n, z_n))

    def x_peer(d):
        return (r, lax.rem(x + d + x_n, x_n), z)

    def owner(d, flip):
        core = k if flip == 0 else 1 - k
        return 2 * lax.rem(y - d + y_n, y_n) + core

    barrier = pltpu.get_barrier_semaphore()
    pl.semaphore_signal(barrier, inc=1, device_id=twin, device_id_type=MESH)
    for d in range(1, y_n):
        pl.semaphore_signal(barrier, inc=1, device_id=y_peer(d), device_id_type=MESH)
    for d in range(1, z_n):
        pl.semaphore_signal(barrier, inc=1, device_id=z_peer(d), device_id_type=MESH)
    for d in range(1, x_n):
        pl.semaphore_signal(barrier, inc=1, device_id=x_peer(d), device_id_type=MESH)
    for d in range(1, y_n):
        there = (2 * lax.rem(y + d, y_n) + 1 - k, x, z)
        pl.semaphore_signal(barrier, inc=1, device_id=there, device_id_type=MESH)

    c = x * z_n + z
    tile = inverses.shape[1]
    count = tile // 2
    lanes = lax.broadcasted_iota(jnp.int32, (2, tile), 1)
    links = couplings[...] * pattern[...].astype(F32)
    links = jnp.where(lanes == tile - 1, 0.0, links)
    swap_rows = swaps[...].astype(F32)
    coef[...] = jnp.zeros_like(coef)
    coef[0:2, :] = pivots[...]
    coef[2:4, :] = links
    coef[4:6, :] = jnp.where(lanes == 0, 0.0, pltpu.roll(links, 1, 1))
    coef[8:12, 0:count] = swap_rows
    table = coef[...].T
    lead_0, partner_0 = swap_rows[0:1], swap_rows[1:2]
    lead_1, partner_1 = swap_rows[2:3], swap_rows[3:4]
    partner_0c, partner_1c = table[:count, 9:10], table[:count, 11:12]
    top = lax.broadcasted_iota(jnp.int32, (2 * tile, 1), 0).astype(F32)
    rows = jnp.concatenate([top, partner_0c, partner_1c], axis=0)
    source = swapped(swapped(rows, lead_1, partner_1), lead_0, partner_0)
    again_c = jnp.sum(jnp.where(partner_0c == partner_1, 1.0, 0.0), axis=1, keepdims=True)
    again_r = jnp.sum(jnp.where(partner_1c == partner_0, 1.0, 0.0), axis=0, keepdims=True)
    partner_col = jnp.concatenate([jnp.where(again_c > 0.0, -1.0, partner_0c), partner_1c], axis=0)
    partner_row = jnp.concatenate([jnp.where(again_r > 0.0, -1.0, partner_0), partner_1], axis=1)
    partner_col = jnp.where(partner_col < 2 * tile, -1.0, partner_col)
    partner_row = jnp.where(partner_row < 2 * tile, -1.0, partner_row)
    columns = lax.broadcasted_iota(jnp.int32, (tile, tile), 1).astype(F32)
    depths = lax.broadcasted_iota(jnp.int32, (tile, tile), 0).astype(F32)
    across = lax.broadcasted_iota(jnp.int32, (3 * tile, tile), 1).astype(F32)

    def first_of(index):
        return (index * tile).astype(F32)

    taken = jnp.zeros((3 * tile, tile), F32)
    for n in range(x_n):
        hit = (source - first_of(r + rows_n * n)) == across
        mark = jnp.where(hit, 1.0, 0.0).astype(BF)
        block = halves(kkt[n * tile : (n + 1) * tile, :])
        taken = taken + dot_n(mark, block[0], NN) + dot_n(mark, block[1], NN)
    for n in range(y_n):
        for core in range(2):
            q = 2 * n + core
            for part in range(3):
                picked[core, n, part * width : (part + 1) * width, :] = taken[
                    part * tile + q * width : part * tile + (q + 1) * width
                ]

    pl.semaphore_wait(barrier, 2 * y_n + z_n + x_n - 3)

    def chip_copy(d):
        n = lax.rem(y + d, y_n)
        return remote(picked.at[1 - k, n], near_in.at[d], p_send.at[d], p_recv.at[d], twin)

    def y_copy(d):
        return remote(
            chip_sum.at[d - 1], far_in.at[d - 1], r_send.at[d - 1], r_recv.at[d - 1], y_peer(d)
        )

    order = [2, 1, 3, 0] if y_n == 4 else list(range(1, y_n)) + [0]
    for d in order:
        chip_copy(d).start()
    for d in order[:-1]:
        chip_copy(d).wait_recv()
        chip_sum[d - 1] = picked[k, lax.rem(y + d, y_n)] + near_in[d]
        y_copy(d).start()
    inv0 = halves(inverses[0].T)
    inv1 = halves(inverses[1].T)
    chip_copy(0).wait_recv()
    total = picked[k, y] + near_in[0]
    for d in range(1, y_n):
        y_copy(d).wait_recv()
        total = total + far_in[d - 1]
    strip[r] = total

    def gather_copy(ref, d, send, recv):
        return remote(ref.at[r], ref.at[r], send.at[d - 1], recv.at[d - 1], y_peer(d))

    def gathered(ref, d, send, recv):
        q = owner(d, 0)
        return remote(ref.at[q], ref.at[q], send.at[d - 1], recv.at[d - 1], y_peer(d))

    def twin_copy(ref, d, flip, send, recv):
        q = owner(d, flip)
        return remote(ref.at[q], ref.at[q], send.at[d], recv.at[d], twin)

    for d in range(1, y_n):
        gather_copy(strip, d, g_send, g_recv).start()
    twin_copy(strip, 0, 0, h_send, h_recv).start()

    offset = lax.rem(z - r + z_n, z_n)
    half = z_n // 2
    is_root = offset == 0
    not_root = jnp.logical_not(is_root)
    upward = offset <= half
    passes = ((offset > 0) & (offset < half)) | (offset > half + 1)
    ahead = jnp.where(upward, 1, z_n - 1)
    reach = jnp.minimum(offset, z_n - offset)
    is_near = reach <= 1
    is_mid = reach == 2
    is_far = reach > 2
    cut = 3 * width // 2
    if y_n == 4:
        turn = [(0, 0), (0, 1), (1, 0), (3, 0), (1, 1), (3, 1), (2, 0), (2, 1)]
    else:
        turn = [(d, flip) for d in range(y_n) for flip in range(2)]
    pieces = 2 * rows_n

    def spot(i):
        q = owner(*turn[i // 2])
        return q, pl.ds((i % 2) * cut, cut)

    def z_copy(src, i, slot, step):
        q, part = spot(i)
        return remote(
            src.at[q, part], wide.at[x, q, part], z_send.at[slot, i], z_recv.at[i], z_peer(step)
        )

    def x_copy(src, i, side):
        q, part = spot(i)
        return remote(
            src.at[q, part],
            wide.at[x, q, part],
            x_send.at[side, i],
            x_recv.at[side, i],
            x_peer(1 if side == 0 else x_n - 1),
        )

    def f_copy(i):
        q, part = spot(i)
        step = 1 if i % 2 == 0 else x_n - 1
        held = wide.at[lax.rem(x + x_n - step, x_n), q, part]
        return remote(held, held, f_send.at[i], f_recv.at[i], x_peer(step))

    def own_piece(i):
        q, part = spot(i)
        d, flip = turn[i // 2]

        @pl.when(is_root)
        def _():
            if i % 2 == 0 and flip == 1:
                twin_copy(strip, d, 1, h_send, h_recv).wait_recv()
            z_copy(strip, i, 0, 1).start()
            z_copy(strip, i, 1, z_n - 1).start()
            x_copy(strip, i, 0).start()
            x_copy(strip, i, 1).start()
            wide[x, q, part] = strip[q, part]

        @pl.when(not_root)
        def _():
            z_copy(wide.at[x], i, 0, ahead).wait_recv()

            @pl.when(passes)
            def _():
                z_copy(wide.at[x], i, 0, ahead).start()

            x_copy(wide.at[x], i, 0).start()
            x_copy(wide.at[x], i, 1).start()

    def side_piece(i):
        for side in (i % 2, 1 - i % 2):
            x_copy(wide.at[x], i, side).wait_recv()
            if side == i % 2:
                f_copy(i).start()

    def share_copy(d):
        return remote(
            shares.at[lax.rem(z + d, z_n)],
            share_in.at[d - 1],
            cz_send.at[d - 1],
            cz_recv.at[d - 1],
            z_peer(d),
        )

    def cross_copy(d):
        return remote(share, cross.at[d - 1], cx_send.at[d - 1], cx_recv.at[d - 1], x_peer(d))

    def share_back(d):
        return remote(
            summed.at[z], summed.at[z], cg_send.at[d - 1], cg_recv.at[d - 1], z_peer(d)
        )

    def share_taken(d):
        q = lax.rem(z - d + z_n, z_n)
        return remote(
            summed.at[q], summed.at[q], cg_send.at[d - 1], cg_recv.at[d - 1], z_peer(d)
        )

    def corner_z():
        value = shares[z]
        for d in range(1, z_n):
            share_copy(d).wait_recv()
            value = value + share_in[d - 1]
        share[...] = value
        for d in range(1, x_n):
            cross_copy(d).start()

    def corner_x():
        value = share[...]
        for d in range(1, x_n):
            cross_copy(d).wait_recv()
            value = value + cross[d - 1]
        summed[z] = value
        for d in range(1, z_n):
            share_back(d).start()

    def corner_back():
        for d in range(1, z_n):
            share_taken(d).wait_recv()
        flat = jnp.concatenate([summed[n] for n in range(z_n)], axis=0)
        corner[r] = flat[: 4 * width]
        special[r] = flat[4 * width :]
        for d in range(1, y_n):
            gather_copy(corner, d, cr_send, cr_recv).start()
        twin_copy(corner, 0, 0, ch_send, ch_recv).start()
        for home in range(2):
            @pl.when((x == 0) & (z == home) & (r != home))
            def _():
                remote(
                    special.at[r], special.at[r], sp_send, sp_recv.at[r], (home, x, z)
                ).start()

    def corner_twin():
        for d in range(1, y_n):
            gathered(corner, d, cr_send, cr_recv).wait_recv()
            twin_copy(corner, d, 0, ch_send, ch_recv).start()

    steps = [corner_z, corner_x, corner_back, corner_twin]
    spots = {True: [[3, 5, 11, 14], [1, 3, 9, 13], [-1, -1, 6, 11]], False: [[2, 3, 5, 6]] * 3}
    spots = spots[pieces == 16]

    def corner_steps(i):
        for kind, at in zip((is_near, is_mid, is_far), spots):
            if i in at:

                @pl.when(kind)
                def _():
                    for step, place in zip(steps, at):
                        if place == i:
                            step()

    @pl.when(is_root)
    def _():
        for i in range(2):
            q, part = spot(i)
            z_copy(strip, i, 0, 1).start()
            z_copy(strip, i, 1, z_n - 1).start()
            x_copy(strip, i, 0).start()
            x_copy(strip, i, 1).start()
            wide[x, q, part] = strip[q, part]

    moves = jnp.where((source - first_of(c)) == across, 1.0, 0.0).astype(BF)
    piece = halves(strip[r])
    part = dot_n(piece[0], moves, NT) + dot_n(piece[1], moves, NT)
    blocks = ((0, 2), (1, 2), (2, 2), (0, 1), (0, 0), (1, 1))
    stacked = jnp.concatenate(
        [
            part[i * width : (i + 1) * width, j * tile : (j + 1) * tile]
            for i, j in blocks
        ],
        axis=0,
    )
    depth = 6 * width // z_n
    for n in range(z_n):
        shares[n] = stacked[n * depth : (n + 1) * depth]
    for d in range(1, z_n):
        share_copy(d).start()

    for d in (1, 3, 2) if y_n == 4 else range(1, y_n):
        gathered(strip, d, g_send, g_recv).wait_recv()
        twin_copy(strip, d, 0, h_send, h_recv).start()

    corner_steps(-1)
    lag = 2
    for i in range(pieces):
        if i > 1:
            own_piece(i)
        else:

            @pl.when(not_root)
            def _():
                z_copy(wide.at[x], i, 0, ahead).wait_recv()

                @pl.when(passes)
                def _():
                    z_copy(wide.at[x], i, 0, ahead).start()

                x_copy(wide.at[x], i, 0).start()
                x_copy(wide.at[x], i, 1).start()

        corner_steps(i)
        if i >= lag:
            side_piece(i - lag)
    for d in range(y_n):
        twin_copy(corner, d, 1, ch_send, ch_recv).wait_recv()

        @pl.when(not_root)
        def _():
            twin_copy(strip, d, 1, h_send, h_recv).wait_recv()

    def along_d(lower_t, panel):
        pivot = table[:, panel : panel + 1]
        after = table[:, 2 + panel : 3 + panel]
        before = table[:, 4 + panel : 5 + panel]
        return (
            lower_t * pivot
            + pltpu.roll(lower_t, tile - 1, 0) * after
            + pltpu.roll(lower_t, 1, 0) * before
        )

    def rows_of(ref, part):
        return jnp.concatenate(
            [ref[q, part * width : (part + 1) * width, :] for q in range(rows_n)], axis=0
        )

    block_01 = rows_of(corner, 3)
    low0_1 = dot3(inv0, halves(block_01))
    scaled0_1 = along_d(low0_1, 0)
    scaled0_1_rows = halves(scaled0_1.T)
    to_partner = [halves(rows_of(corner, part)) for part in range(3)]

    def panels(ref, index):
        hit = (partner_col - first_of(index)) == columns
        mark = jnp.where(hit, 1.0, 0.0).astype(BF)
        keep = 1.0 - jnp.sum(jnp.where(hit, 1.0, 0.0), axis=0, keepdims=True)
        fixed = [
            rows_of(ref, part) * keep
            + dot_n(to_partner[part][0], mark, NN)
            + dot_n(to_partner[part][1], mark, NN)
            for part in range(3)
        ]
        upper = jnp.where(index == 1, block_01, fixed[0])
        low0 = dot3(inv0, halves(upper)) * jnp.where(index > 0, 1.0, 0.0)
        below = fixed[1] - dot3(scaled0_1_rows, halves(low0))
        low1 = dot3(inv1, halves(below)) * jnp.where(index > 1, 1.0, 0.0)
        return low0, low1, fixed[2], mark, keep

    low0_c, low1_c, moved_c, mark_c, keep_c = panels(strip, c)
    scaled0 = along_d(low0_c, 0)
    scaled1 = along_d(low1_c, 1)
    scaled0_rows = halves(scaled0.T)
    scaled1_rows = halves(scaled1.T)
    moved_rows = halves(moved_c.T)
    hit_c = (partner_row - first_of(c)) == depths
    mark_rows = jnp.where(hit_c, 1.0, 0.0).astype(BF)

    def slot_rows(slot):
        index = r + rows_n * slot
        low0, low1, moved, mark, keep = panels(wide.at[slot], index)
        place = pl.ds(pl.multiple_of(slot * tile, tile), tile)

        @pl.when(c > 1)
        def _():
            hit = (partner_row - first_of(index)) == depths
            keep_rows = 1.0 - jnp.sum(jnp.where(hit, 1.0, 0.0), axis=1, keepdims=True)
            moved_h = halves(moved * keep)
            change = dot_n(moved_rows[0], mark, NN) + dot_n(moved_rows[1], mark, NN)
            change = change + dot_n(mark_rows, moved_h[0], NN) + dot_n(mark_rows, moved_h[1], NN)
            change = change - dot3(scaled0_rows, halves(low0))
            change = change - dot3(scaled1_rows, halves(low1))
            value = kkt[place, :] * keep_rows * keep_c + change.T
            out[place, :] = jnp.where(
                index == 0, scaled0, jnp.where(index == 1, scaled1, value)
            )

        @pl.when(c == 0)
        def _():
            out[place, :] = jnp.where(index == 0, rows_of(special, 0), low0.T)

        @pl.when(c == 1)
        def _():
            first = rows_of(special, 1) - dot3(scaled0_1_rows, halves(low0_1)).T
            value = jnp.where(index == 1, first, low1.T)
            out[place, :] = jnp.where(index == 0, scaled0_1, value)

    for i in range(pieces - lag, pieces):
        side_piece(i)

    for home in range(2):
        for n in range(rows_n):
            if n != home:

                @pl.when((x == 0) & (z == home) & (r == home))
                def _():
                    remote(
                        special.at[n], special.at[n], sp_send, sp_recv.at[n], (n, x, z)
                    ).wait_recv()

    for step in (0, 1, 3):
        slot_rows(lax.rem(x + step, x_n))
    for i in range(pieces):
        f_copy(i).wait()
    slot_rows(lax.rem(x + 2, x_n))

    for d in range(y_n):
        twin_copy(strip, d, 0, h_send, h_recv).wait_send()
        twin_copy(corner, d, 0, ch_send, ch_recv).wait_send()
        chip_copy(d).wait_send()
    for d in range(1, y_n):
        y_copy(d).wait_send()
        gather_copy(strip, d, g_send, g_recv).wait_send()
        gather_copy(corner, d, cr_send, cr_recv).wait_send()
    for i in range(pieces):
        x_copy(wide.at[x], i, 0).wait_send()
        x_copy(wide.at[x], i, 1).wait_send()

        @pl.when(is_root | passes)
        def _():
            z_copy(wide.at[x], i, 0, ahead).wait_send()

        @pl.when(is_root)
        def _():
            z_copy(wide.at[x], i, 1, ahead).wait_send()

    for d in range(1, z_n):
        share_copy(d).wait_send()
        share_back(d).wait_send()
    for d in range(1, x_n):
        cross_copy(d).wait_send()
    for home in range(2):
        for n in range(rows_n):
            if n != home:
                here = (x == 0) & (z == home)

                @pl.when(here & (r == n))
                def _():
                    remote(
                        special.at[n], special.at[n], sp_send, sp_recv.at[n], (home, x, z)
                    ).wait_send()


def shards(kkt, swaps, inverses, pivots, couplings, pattern):
    tile = inverses.shape[1]
    rows_n = lax.axis_size("row")
    x_n = lax.axis_size("col_0")
    z_n = lax.axis_size("col_1")
    y_n = rows_n // 2
    width = tile // rows_n
    depth = 6 * width // z_n
    dma = pltpu.SemaphoreType.DMA
    vmem = pl.BlockSpec(memory_space=pltpu.VMEM)
    return pl.pallas_call(
        functools.partial(step_kernel, (y_n, x_n, z_n, width)),
        out_shape=jax.ShapeDtypeStruct(kkt.shape, F32),
        in_specs=[vmem] * 6,
        out_specs=vmem,
        scratch_shapes=[
            pltpu.VMEM((128, tile), F32),
            pltpu.VMEM((2, y_n, 3 * width, tile), F32),
            pltpu.VMEM((rows_n, 3 * width, tile), F32),
            pltpu.VMEM((x_n, rows_n, 3 * width, tile), F32),
            pltpu.VMEM((rows_n, 4 * width, tile), F32),
            pltpu.VMEM((rows_n, 2 * width, tile), F32),
            pltpu.VMEM((y_n, 3 * width, tile), F32),
            pltpu.VMEM((y_n - 1, 3 * width, tile), F32),
            pltpu.VMEM((y_n - 1, 3 * width, tile), F32),
            pltpu.VMEM((z_n, depth, tile), F32),
            pltpu.VMEM((depth, tile), F32),
            pltpu.VMEM((z_n - 1, depth, tile), F32),
            pltpu.VMEM((x_n - 1, depth, tile), F32),
            pltpu.VMEM((z_n, depth, tile), F32),
            dma((y_n,)),
            dma((y_n,)),
            dma((y_n - 1,)),
            dma((y_n - 1,)),
            dma((y_n - 1,)),
            dma((y_n - 1,)),
            dma((y_n,)),
            dma((y_n,)),
            dma((2, 2 * rows_n)),
            dma((2 * rows_n,)),
            dma((2, 2 * rows_n)),
            dma((2, 2 * rows_n)),
            dma((2 * rows_n,)),
            dma((2 * rows_n,)),
            dma((z_n - 1,)),
            dma((z_n - 1,)),
            dma((x_n - 1,)),
            dma((x_n - 1,)),
            dma((z_n - 1,)),
            dma((z_n - 1,)),
            dma((y_n - 1,)),
            dma((y_n - 1,)),
            dma((y_n,)),
            dma((y_n,)),
            dma,
            dma((rows_n,)),
        ],
        compiler_params=pltpu.CompilerParams(collective_id=0, has_side_effects=True),
    )(kkt, swaps.reshape(4, -1), inverses, pivots, couplings, pattern)


def solution(mesh):
    z_size = mesh.shape["row"]
    finer = Mesh(mesh.devices.reshape(mesh.shape["row"], -1, z_size), ("row", "col_0", "col_1"))
    in_specs = (P("row", COL), P(), P(), P(), P(), P())
    return jax.shard_map(
        shards, mesh=finer, in_specs=in_specs, out_specs=P("row", COL), check_vma=False
    )
```

```python
import functools

import jax
import jax.numpy as jnp
from jax import lax
from jax.experimental import pallas as pl
from jax.experimental.pallas import tpu as pltpu
from jax.sharding import Mesh
from jax.sharding import PartitionSpec as P

COL = ("col_0", "col_1")
BF = jnp.bfloat16
F32 = jnp.float32
NN = ((1,), (0,))
NT = ((1,), (1,))


def halves(a):
    high = a.astype(BF)
    return high, (a - high.astype(F32)).astype(BF)


def dot_n(a, b, dims):
    return lax.dot_general(a, b, (dims, ((), ())), preferred_element_type=F32)


def dot3(a, b):
    return dot_n(a[0], b[0], NN) + (dot_n(a[0], b[1], NN) + dot_n(a[1], b[0], NN))


def swapped(rows, lead, partner):
    to_partner = rows == lead
    to_lead = rows == partner
    moved = jnp.where(to_partner, partner, 0.0) + jnp.where(to_lead, lead, 0.0)
    touched = jnp.where(to_partner | to_lead, 1.0, 0.0)
    moved = jnp.sum(moved, axis=1, keepdims=True)
    return jnp.where(jnp.sum(touched, axis=1, keepdims=True) > 0.0, moved, rows)


MESH = pl.DeviceIdType.MESH


def remote(src, dst, send, recv, device):
    return pltpu.make_async_remote_copy(
        src_ref=src, dst_ref=dst, send_sem=send, recv_sem=recv, device_id=device, device_id_type=MESH
    )


def step_kernel(
    sizes,
    kkt,
    swaps,
    inverses,
    pivots,
    couplings,
    pattern,
    out,
    coef,
    picked,
    strip,
    wide,
    corner,
    special,
    near_in,
    chip_sum,
    far_in,
    shares,
    share,
    share_in,
    cross,
    summed,
    p_send,
    p_recv,
    r_send,
    r_recv,
    g_send,
    g_recv,
    h_send,
    h_recv,
    z_send,
    z_recv,
    x_send,
    x_recv,
    f_send,
    f_recv,
    cz_send,
    cz_recv,
    cx_send,
    cx_recv,
    cg_send,
    cg_recv,
    cr_send,
    cr_recv,
    ch_send,
    ch_recv,
    sp_send,
    sp_recv,
):
    y_n, x_n, z_n, width = sizes
    rows_n = 2 * y_n
    r = lax.axis_index("row")
    x = lax.axis_index("col_0")
    z = lax.axis_index("col_1")
    y = r // 2
    k = lax.rem(r, 2)
    twin = (r + 1 - 2 * k, x, z)

    def y_peer(d):
        return (lax.rem(r + 2 * d, rows_n), x, z)

    def z_peer(d):
        return (r, x, lax.rem(z + d + z_n, z_n))

    def x_peer(d):
        return (r, lax.rem(x + d + x_n, x_n), z)

    def owner(d, flip):
        core = k if flip == 0 else 1 - k
        return 2 * lax.rem(y - d + y_n, y_n) + core

    barrier = pltpu.get_barrier_semaphore()
    pl.semaphore_signal(barrier, inc=1, device_id=twin, device_id_type=MESH)
    for d in range(1, y_n):
        pl.semaphore_signal(barrier, inc=1, device_id=y_peer(d), device_id_type=MESH)
    for d in range(1, z_n):
        pl.semaphore_signal(barrier, inc=1, device_id=z_peer(d), device_id_type=MESH)
    for d in range(1, x_n):
        pl.semaphore_signal(barrier, inc=1, device_id=x_peer(d), device_id_type=MESH)
    for d in range(1, y_n):
        there = (2 * lax.rem(y + d, y_n) + 1 - k, x, z)
        pl.semaphore_signal(barrier, inc=1, device_id=there, device_id_type=MESH)

    c = x * z_n + z
    tile = inverses.shape[1]
    count = tile // 2
    lanes = lax.broadcasted_iota(jnp.int32, (2, tile), 1)
    links = couplings[...] * pattern[...].astype(F32)
    links = jnp.where(lanes == tile - 1, 0.0, links)
    swap_rows = swaps[...].astype(F32)
    coef[...] = jnp.zeros_like(coef)
    coef[0:2, :] = pivots[...]
    coef[2:4, :] = links
    coef[4:6, :] = jnp.where(lanes == 0, 0.0, pltpu.roll(links, 1, 1))
    coef[8:12, 0:count] = swap_rows
    table = coef[...].T
    lead_0, partner_0 = swap_rows[0:1], swap_rows[1:2]
    lead_1, partner_1 = swap_rows[2:3], swap_rows[3:4]
    partner_0c, partner_1c = table[:count, 9:10], table[:count, 11:12]
    top = lax.broadcasted_iota(jnp.int32, (2 * tile, 1), 0).astype(F32)
    rows = jnp.concatenate([top, partner_0c, partner_1c], axis=0)
    source = swapped(swapped(rows, lead_1, partner_1), lead_0, partner_0)
    again_c = jnp.sum(jnp.where(partner_0c == partner_1, 1.0, 0.0), axis=1, keepdims=True)
    again_r = jnp.sum(jnp.where(partner_1c == partner_0, 1.0, 0.0), axis=0, keepdims=True)
    partner_col = jnp.concatenate([jnp.where(again_c > 0.0, -1.0, partner_0c), partner_1c], axis=0)
    partner_row = jnp.concatenate([jnp.where(again_r > 0.0, -1.0, partner_0), partner_1], axis=1)
    partner_col = jnp.where(partner_col < 2 * tile, -1.0, partner_col)
    partner_row = jnp.where(partner_row < 2 * tile, -1.0, partner_row)
    columns = lax.broadcasted_iota(jnp.int32, (tile, tile), 1).astype(F32)
    depths = lax.broadcasted_iota(jnp.int32, (tile, tile), 0).astype(F32)
    across = lax.broadcasted_iota(jnp.int32, (3 * tile, tile), 1).astype(F32)

    def first_of(index):
        return (index * tile).astype(F32)

    taken = jnp.zeros((3 * tile, tile), F32)
    for n in range(x_n):
        hit = (source - first_of(r + rows_n * n)) == across
        mark = jnp.where(hit, 1.0, 0.0).astype(BF)
        block = halves(kkt[n * tile : (n + 1) * tile, :])
        taken = taken + dot_n(mark, block[0], NN) + dot_n(mark, block[1], NN)
    for n in range(y_n):
        for core in range(2):
            q = 2 * n + core
            for part in range(3):
                picked[core, n, part * width : (part + 1) * width, :] = taken[
                    part * tile + q * width : part * tile + (q + 1) * width
                ]

    pl.semaphore_wait(barrier, 2 * y_n + z_n + x_n - 3)

    def chip_copy(d):
        n = lax.rem(y + d, y_n)
        return remote(picked.at[1 - k, n], near_in.at[d], p_send.at[d], p_recv.at[d], twin)

    cut = 3 * width // 2

    def y_copy(d, half):
        part = pl.ds(half * cut, cut)
        return remote(
            chip_sum.at[d - 1, part],
            far_in.at[d - 1, part],
            r_send.at[half, d - 1],
            r_recv.at[half, d - 1],
            y_peer(d),
        )

    order = [2, 1, 3, 0] if y_n == 4 else list(range(1, y_n)) + [0]
    for d in order:
        chip_copy(d).start()
    for d in order[:-1]:
        chip_copy(d).wait_recv()
        chip_sum[d - 1] = picked[k, lax.rem(y + d, y_n)] + near_in[d]
        y_copy(d, 0).start()
    for d in order[:-1]:
        y_copy(d, 1).start()
    inv0 = halves(inverses[0].T)
    inv1 = halves(inverses[1].T)
    chip_copy(0).wait_recv()

    def gather_copy(ref, d, send, recv):
        return remote(ref.at[r], ref.at[r], send.at[d - 1], recv.at[d - 1], y_peer(d))

    def gathered(ref, d, send, recv):
        q = owner(d, 0)
        return remote(ref.at[q], ref.at[q], send.at[d - 1], recv.at[d - 1], y_peer(d))

    def twin_copy(ref, d, flip, send, recv):
        q = owner(d, flip)
        return remote(ref.at[q], ref.at[q], send.at[d], recv.at[d], twin)

    offset = lax.rem(z - r + z_n, z_n)
    half = z_n // 2
    is_root = offset == 0
    not_root = jnp.logical_not(is_root)
    upward = offset <= half
    passes = ((offset > 0) & (offset < half)) | (offset > half + 1)
    ahead = jnp.where(upward, 1, z_n - 1)
    reach = jnp.minimum(offset, z_n - offset)
    is_near = reach <= 1
    is_mid = reach == 2
    is_far = reach > 2
    if y_n == 4:
        turn = [(0, 0), (0, 1), (1, 0), (3, 0), (1, 1), (3, 1), (2, 0), (2, 1)]
    else:
        turn = [(d, flip) for d in range(y_n) for flip in range(2)]
    spans = []
    for e in range(rows_n):
        count_e = 4 if e in (0, rows_n - 1) else 2
        depth_e = 3 * width // count_e
        spans += [(e, n * depth_e, depth_e) for n in range(count_e)]
    pieces = len(spans)

    def spot(i):
        e, start, size = spans[i]
        return owner(*turn[e]), pl.ds(start, size)

    def z_copy(src, i, slot, step):
        q, part = spot(i)
        return remote(
            src.at[q, part], wide.at[x, q, part], z_send.at[slot, i], z_recv.at[i], z_peer(step)
        )

    def x_copy(src, i, side):
        q, part = spot(i)
        return remote(
            src.at[q, part],
            wide.at[x, q, part],
            x_send.at[side, i],
            x_recv.at[side, i],
            x_peer(1 if side == 0 else x_n - 1),
        )

    def f_copy(i):
        q, part = spot(i)
        step = 1 if i % 2 == 0 else x_n - 1
        held = wide.at[lax.rem(x + x_n - step, x_n), q, part]
        return remote(held, held, f_send.at[i], f_recv.at[i], x_peer(step))

    def own_piece(i):
        q, part = spot(i)
        d, flip = turn[spans[i][0]]

        @pl.when(is_root)
        def _():
            if spans[i][1] == 0 and flip == 1:
                twin_copy(strip, d, 1, h_send, h_recv).wait_recv()
            z_copy(strip, i, 0, 1).start()
            z_copy(strip, i, 1, z_n - 1).start()
            x_copy(strip, i, 0).start()
            x_copy(strip, i, 1).start()
            wide[x, q, part] = strip[q, part]

        @pl.when(not_root)
        def _():
            z_copy(wide.at[x], i, 0, ahead).wait_recv()

            @pl.when(passes)
            def _():
                z_copy(wide.at[x], i, 0, ahead).start()

            x_copy(wide.at[x], i, 0).start()
            x_copy(wide.at[x], i, 1).start()

    def side_piece(i):
        for side in (i % 2, 1 - i % 2):
            x_copy(wide.at[x], i, side).wait_recv()
            if side == i % 2:
                f_copy(i).start()

    def share_copy(d):
        return remote(
            shares.at[lax.rem(z + d, z_n)],
            share_in.at[d - 1],
            cz_send.at[d - 1],
            cz_recv.at[d - 1],
            z_peer(d),
        )

    def cross_copy(d):
        return remote(share, cross.at[d - 1], cx_send.at[d - 1], cx_recv.at[d - 1], x_peer(d))

    def share_back(d):
        return remote(
            summed.at[z], summed.at[z], cg_send.at[d - 1], cg_recv.at[d - 1], z_peer(d)
        )

    def share_taken(d):
        q = lax.rem(z - d + z_n, z_n)
        return remote(
            summed.at[q], summed.at[q], cg_send.at[d - 1], cg_recv.at[d - 1], z_peer(d)
        )

    def corner_z():
        value = shares[z]
        for d in range(1, z_n):
            share_copy(d).wait_recv()
            value = value + share_in[d - 1]
        share[...] = value
        for d in range(1, x_n):
            cross_copy(d).start()

    def corner_x():
        value = share[...]
        for d in range(1, x_n):
            cross_copy(d).wait_recv()
            value = value + cross[d - 1]
        summed[z] = value
        for d in range(1, z_n):
            share_back(d).start()

    def corner_back():
        for d in range(1, z_n):
            share_taken(d).wait_recv()
        flat = jnp.concatenate([summed[n] for n in range(z_n)], axis=0)
        corner[r] = flat[: 4 * width]
        special[r] = flat[4 * width :]
        for d in range(1, y_n):
            gather_copy(corner, d, cr_send, cr_recv).start()
        twin_copy(corner, 0, 0, ch_send, ch_recv).start()
        for home in range(2):
            @pl.when((x == 0) & (z == home) & (r != home))
            def _():
                remote(
                    special.at[r], special.at[r], sp_send, sp_recv.at[r], (home, x, z)
                ).start()

    def corner_twin():
        for d in range(1, y_n):
            gathered(corner, d, cr_send, cr_recv).wait_recv()
            twin_copy(corner, d, 0, ch_send, ch_recv).start()

    steps = [corner_z, corner_x, corner_back, corner_twin]
    spots = [[5, 7, 13, 15], [3, 5, 11, 15], [-1, -1, 8, 13]]
    if y_n != 4:
        spots = [[2, 3, 5, 6]] * 3

    def corner_steps(i):
        for kind, at in zip((is_near, is_mid, is_far), spots):
            if i in at:

                @pl.when(kind)
                def _():
                    for step, place in zip(steps, at):
                        if place == i:
                            step()

    for half in range(2):
        rows_h = slice(half * cut, (half + 1) * cut)
        total = picked[k, y, rows_h, :] + near_in[0, rows_h, :]
        for d in range(1, y_n):
            y_copy(d, half).wait_recv()
            total = total + far_in[d - 1, rows_h, :]
        strip[r, rows_h, :] = total

        @pl.when(is_root)
        def _():
            for i in (2 * half, 2 * half + 1):
                q, part = spot(i)
                z_copy(strip, i, 0, 1).start()
                z_copy(strip, i, 1, z_n - 1).start()
                x_copy(strip, i, 0).start()
                x_copy(strip, i, 1).start()
                wide[x, q, part] = strip[q, part]

    for d in range(1, y_n):
        gather_copy(strip, d, g_send, g_recv).start()
    twin_copy(strip, 0, 0, h_send, h_recv).start()

    moves = jnp.where((source - first_of(c)) == across, 1.0, 0.0).astype(BF)
    piece = halves(strip[r])
    part = dot_n(piece[0], moves, NT) + dot_n(piece[1], moves, NT)
    blocks = ((0, 2), (1, 2), (2, 2), (0, 1), (0, 0), (1, 1))
    stacked = jnp.concatenate(
        [
            part[i * width : (i + 1) * width, j * tile : (j + 1) * tile]
            for i, j in blocks
        ],
        axis=0,
    )
    depth = 6 * width // z_n
    for n in range(z_n):
        shares[n] = stacked[n * depth : (n + 1) * depth]
    for d in range(1, z_n):
        share_copy(d).start()

    for d in (1, 3, 2) if y_n == 4 else range(1, y_n):
        gathered(strip, d, g_send, g_recv).wait_recv()
        twin_copy(strip, d, 0, h_send, h_recv).start()

    corner_steps(-1)
    lag = 5
    for i in range(pieces):
        if i > 3:
            own_piece(i)
        else:

            @pl.when(not_root)
            def _():
                z_copy(wide.at[x], i, 0, ahead).wait_recv()

                @pl.when(passes)
                def _():
                    z_copy(wide.at[x], i, 0, ahead).start()

                x_copy(wide.at[x], i, 0).start()
                x_copy(wide.at[x], i, 1).start()

        corner_steps(i)
        if i >= lag:
            side_piece(i - lag)
    for d in range(y_n):
        twin_copy(corner, d, 1, ch_send, ch_recv).wait_recv()

        @pl.when(not_root)
        def _():
            twin_copy(strip, d, 1, h_send, h_recv).wait_recv()

    def along_d(lower_t, panel):
        pivot = table[:, panel : panel + 1]
        after = table[:, 2 + panel : 3 + panel]
        before = table[:, 4 + panel : 5 + panel]
        return (
            lower_t * pivot
            + pltpu.roll(lower_t, tile - 1, 0) * after
            + pltpu.roll(lower_t, 1, 0) * before
        )

    def rows_of(ref, part):
        return jnp.concatenate(
            [ref[q, part * width : (part + 1) * width, :] for q in range(rows_n)], axis=0
        )

    block_01 = rows_of(corner, 3)
    low0_1 = dot3(inv0, halves(block_01))
    scaled0_1 = along_d(low0_1, 0)
    scaled0_1_rows = halves(scaled0_1.T)
    to_partner = [halves(rows_of(corner, part)) for part in range(3)]

    def panels(ref, index):
        hit = (partner_col - first_of(index)) == columns
        mark = jnp.where(hit, 1.0, 0.0).astype(BF)
        keep = 1.0 - jnp.sum(jnp.where(hit, 1.0, 0.0), axis=0, keepdims=True)
        fixed = [
            rows_of(ref, part) * keep
            + dot_n(to_partner[part][0], mark, NN)
            + dot_n(to_partner[part][1], mark, NN)
            for part in range(3)
        ]
        upper = jnp.where(index == 1, block_01, fixed[0])
        low0 = dot3(inv0, halves(upper)) * jnp.where(index > 0, 1.0, 0.0)
        below = fixed[1] - dot3(scaled0_1_rows, halves(low0))
        low1 = dot3(inv1, halves(below)) * jnp.where(index > 1, 1.0, 0.0)
        return low0, low1, fixed[2], mark, keep

    low0_c, low1_c, moved_c, mark_c, keep_c = panels(strip, c)
    scaled0 = along_d(low0_c, 0)
    scaled1 = along_d(low1_c, 1)
    scaled0_rows = halves(scaled0.T)
    scaled1_rows = halves(scaled1.T)
    moved_rows = halves(moved_c.T)
    hit_c = (partner_row - first_of(c)) == depths
    mark_rows = jnp.where(hit_c, 1.0, 0.0).astype(BF)

    def slot_rows(slot):
        index = r + rows_n * slot
        low0, low1, moved, mark, keep = panels(wide.at[slot], index)
        place = pl.ds(pl.multiple_of(slot * tile, tile), tile)

        @pl.when(c > 1)
        def _():
            hit = (partner_row - first_of(index)) == depths
            keep_rows = 1.0 - jnp.sum(jnp.where(hit, 1.0, 0.0), axis=1, keepdims=True)
            moved_h = halves(moved * keep)
            change = dot_n(moved_rows[0], mark, NN) + dot_n(moved_rows[1], mark, NN)
            change = change + dot_n(mark_rows, moved_h[0], NN) + dot_n(mark_rows, moved_h[1], NN)
            change = change - dot3(scaled0_rows, halves(low0))
            change = change - dot3(scaled1_rows, halves(low1))
            value = kkt[place, :] * keep_rows * keep_c + change.T
            out[place, :] = jnp.where(
                index == 0, scaled0, jnp.where(index == 1, scaled1, value)
            )

        @pl.when(c == 0)
        def _():
            out[place, :] = jnp.where(index == 0, rows_of(special, 0), low0.T)

        @pl.when(c == 1)
        def _():
            first = rows_of(special, 1) - dot3(scaled0_1_rows, halves(low0_1)).T
            value = jnp.where(index == 1, first, low1.T)
            out[place, :] = jnp.where(index == 0, scaled0_1, value)

    for home in range(2):
        for n in range(rows_n):
            if n != home:

                @pl.when((x == 0) & (z == home) & (r == home))
                def _():
                    remote(
                        special.at[n], special.at[n], sp_send, sp_recv.at[n], (n, x, z)
                    ).wait_recv()

    side_piece(pieces - 5)
    side_piece(pieces - 4)
    slot_rows(x)
    for i in range(pieces - 3, pieces):
        side_piece(i)

    for step in (1, 3):
        slot_rows(lax.rem(x + step, x_n))
    for i in range(pieces):
        f_copy(i).wait()
    slot_rows(lax.rem(x + 2, x_n))

    for d in range(y_n):
        twin_copy(strip, d, 0, h_send, h_recv).wait_send()
        twin_copy(corner, d, 0, ch_send, ch_recv).wait_send()
        chip_copy(d).wait_send()
    for d in range(1, y_n):
        y_copy(d, 0).wait_send()
        y_copy(d, 1).wait_send()
        gather_copy(strip, d, g_send, g_recv).wait_send()
        gather_copy(corner, d, cr_send, cr_recv).wait_send()
    for i in range(pieces):
        x_copy(wide.at[x], i, 0).wait_send()
        x_copy(wide.at[x], i, 1).wait_send()

        @pl.when(is_root | passes)
        def _():
            z_copy(wide.at[x], i, 0, ahead).wait_send()

        @pl.when(is_root)
        def _():
            z_copy(wide.at[x], i, 1, ahead).wait_send()

    for d in range(1, z_n):
        share_copy(d).wait_send()
        share_back(d).wait_send()
    for d in range(1, x_n):
        cross_copy(d).wait_send()
    for home in range(2):
        for n in range(rows_n):
            if n != home:
                here = (x == 0) & (z == home)

                @pl.when(here & (r == n))
                def _():
                    remote(
                        special.at[n], special.at[n], sp_send, sp_recv.at[n], (home, x, z)
                    ).wait_send()


def shards(kkt, swaps, inverses, pivots, couplings, pattern):
    tile = inverses.shape[1]
    rows_n = lax.axis_size("row")
    x_n = lax.axis_size("col_0")
    z_n = lax.axis_size("col_1")
    y_n = rows_n // 2
    width = tile // rows_n
    depth = 6 * width // z_n
    dma = pltpu.SemaphoreType.DMA
    vmem = pl.BlockSpec(memory_space=pltpu.VMEM)
    return pl.pallas_call(
        functools.partial(step_kernel, (y_n, x_n, z_n, width)),
        out_shape=jax.ShapeDtypeStruct(kkt.shape, F32),
        in_specs=[vmem] * 6,
        out_specs=vmem,
        scratch_shapes=[
            pltpu.VMEM((128, tile), F32),
            pltpu.VMEM((2, y_n, 3 * width, tile), F32),
            pltpu.VMEM((rows_n, 3 * width, tile), F32),
            pltpu.VMEM((x_n, rows_n, 3 * width, tile), F32),
            pltpu.VMEM((rows_n, 4 * width, tile), F32),
            pltpu.VMEM((rows_n, 2 * width, tile), F32),
            pltpu.VMEM((y_n, 3 * width, tile), F32),
            pltpu.VMEM((y_n - 1, 3 * width, tile), F32),
            pltpu.VMEM((y_n - 1, 3 * width, tile), F32),
            pltpu.VMEM((z_n, depth, tile), F32),
            pltpu.VMEM((depth, tile), F32),
            pltpu.VMEM((z_n - 1, depth, tile), F32),
            pltpu.VMEM((x_n - 1, depth, tile), F32),
            pltpu.VMEM((z_n, depth, tile), F32),
            dma((y_n,)),
            dma((y_n,)),
            dma((2, y_n - 1)),
            dma((2, y_n - 1)),
            dma((y_n - 1,)),
            dma((y_n - 1,)),
            dma((y_n,)),
            dma((y_n,)),
            dma((2, 2 * rows_n + 4)),
            dma((2 * rows_n + 4,)),
            dma((2, 2 * rows_n + 4)),
            dma((2, 2 * rows_n + 4)),
            dma((2 * rows_n + 4,)),
            dma((2 * rows_n + 4,)),
            dma((z_n - 1,)),
            dma((z_n - 1,)),
            dma((x_n - 1,)),
            dma((x_n - 1,)),
            dma((z_n - 1,)),
            dma((z_n - 1,)),
            dma((y_n - 1,)),
            dma((y_n - 1,)),
            dma((y_n,)),
            dma((y_n,)),
            dma,
            dma((rows_n,)),
        ],
        compiler_params=pltpu.CompilerParams(
            collective_id=0, has_side_effects=True, vmem_limit_bytes=32 << 20
        ),
    )(kkt, swaps.reshape(4, -1), inverses, pivots, couplings, pattern)


def solution(mesh):
    z_size = mesh.shape["row"]
    finer = Mesh(mesh.devices.reshape(mesh.shape["row"], -1, z_size), ("row", "col_0", "col_1"))
    in_specs = (P("row", COL), P(), P(), P(), P(), P())
    return jax.shard_map(
        shards, mesh=finer, in_specs=in_specs, out_specs=P("row", COL), check_vma=False
    )
```

```python
import functools

import jax
import jax.numpy as jnp
from jax import lax
from jax.experimental import pallas as pl
from jax.experimental.pallas import tpu as pltpu
from jax.sharding import Mesh
from jax.sharding import PartitionSpec as P

COL = ("col_0", "col_1")
BF = jnp.bfloat16
F32 = jnp.float32
NN = ((1,), (0,))
NT = ((1,), (1,))


def halves(a):
    high = a.astype(BF)
    return high, (a - high.astype(F32)).astype(BF)


def dot_n(a, b, dims):
    return lax.dot_general(a, b, (dims, ((), ())), preferred_element_type=F32)


def dot3(a, b):
    return dot_n(a[0], b[0], NN) + (dot_n(a[0], b[1], NN) + dot_n(a[1], b[0], NN))


def swapped(rows, lead, partner):
    to_partner = rows == lead
    to_lead = rows == partner
    moved = jnp.where(to_partner, partner, 0.0) + jnp.where(to_lead, lead, 0.0)
    touched = jnp.where(to_partner | to_lead, 1.0, 0.0)
    moved = jnp.sum(moved, axis=1, keepdims=True)
    return jnp.where(jnp.sum(touched, axis=1, keepdims=True) > 0.0, moved, rows)


MESH = pl.DeviceIdType.MESH


def remote(src, dst, send, recv, device):
    return pltpu.make_async_remote_copy(
        src_ref=src, dst_ref=dst, send_sem=send, recv_sem=recv, device_id=device, device_id_type=MESH
    )


def step_kernel(
    sizes,
    kkt_hbm,
    swaps_hbm,
    inverses_hbm,
    pivots_hbm,
    couplings_hbm,
    pattern_hbm,
    out,
    kkt,
    swaps,
    inverses,
    pivots,
    couplings,
    pattern,
    in_sem,
    coef,
    picked,
    strip,
    wide,
    corner,
    special,
    near_in,
    chip_sum,
    far_in,
    shares,
    share,
    share_in,
    cross,
    summed,
    p_send,
    p_recv,
    r_send,
    r_recv,
    g_send,
    g_recv,
    h_send,
    h_recv,
    z_send,
    z_recv,
    x_send,
    x_recv,
    f_send,
    f_recv,
    cz_send,
    cz_recv,
    cx_send,
    cx_recv,
    cg_send,
    cg_recv,
    cr_send,
    cr_recv,
    ch_send,
    ch_recv,
    sp_send,
    sp_recv,
):
    y_n, x_n, z_n, width = sizes
    rows_n = 2 * y_n
    r = lax.axis_index("row")
    x = lax.axis_index("col_0")
    z = lax.axis_index("col_1")
    y = r // 2
    k = lax.rem(r, 2)
    twin = (r + 1 - 2 * k, x, z)

    def y_peer(d):
        return (lax.rem(r + 2 * d, rows_n), x, z)

    def z_peer(d):
        return (r, x, lax.rem(z + d + z_n, z_n))

    def x_peer(d):
        return (r, lax.rem(x + d + x_n, x_n), z)

    def owner(d, flip):
        core = k if flip == 0 else 1 - k
        return 2 * lax.rem(y - d + y_n, y_n) + core

    loads = [
        pltpu.make_async_copy(src, dst, in_sem.at[n])
        for n, (src, dst) in enumerate(
            (
                (swaps_hbm, swaps),
                (pivots_hbm, pivots),
                (couplings_hbm, couplings),
                (pattern_hbm, pattern),
                (kkt_hbm, kkt),
                (inverses_hbm, inverses),
            )
        )
    ]
    for load in loads:
        load.start()
    barrier = pltpu.get_barrier_semaphore()
    pl.semaphore_signal(barrier, inc=1, device_id=twin, device_id_type=MESH)
    for d in range(1, y_n):
        pl.semaphore_signal(barrier, inc=1, device_id=y_peer(d), device_id_type=MESH)
    for d in range(1, z_n):
        pl.semaphore_signal(barrier, inc=1, device_id=z_peer(d), device_id_type=MESH)
    for d in range(1, x_n):
        pl.semaphore_signal(barrier, inc=1, device_id=x_peer(d), device_id_type=MESH)
    for d in range(1, y_n):
        there = (2 * lax.rem(y + d, y_n) + 1 - k, x, z)
        pl.semaphore_signal(barrier, inc=1, device_id=there, device_id_type=MESH)

    c = x * z_n + z
    tile = inverses.shape[1]
    for load in loads[:4]:
        load.wait()
    count = tile // 2
    lanes = lax.broadcasted_iota(jnp.int32, (2, tile), 1)
    links = couplings[...] * pattern[...].astype(F32)
    links = jnp.where(lanes == tile - 1, 0.0, links)
    swap_rows = swaps[...].astype(F32)
    coef[...] = jnp.zeros_like(coef)
    coef[0:2, :] = pivots[...]
    coef[2:4, :] = links
    coef[4:6, :] = jnp.where(lanes == 0, 0.0, pltpu.roll(links, 1, 1))
    coef[8:12, 0:count] = swap_rows
    table = coef[...].T
    lead_0, partner_0 = swap_rows[0:1], swap_rows[1:2]
    lead_1, partner_1 = swap_rows[2:3], swap_rows[3:4]
    partner_0c, partner_1c = table[:count, 9:10], table[:count, 11:12]
    top = lax.broadcasted_iota(jnp.int32, (2 * tile, 1), 0).astype(F32)
    rows = jnp.concatenate([top, partner_0c, partner_1c], axis=0)
    source = swapped(swapped(rows, lead_1, partner_1), lead_0, partner_0)
    again_c = jnp.sum(jnp.where(partner_0c == partner_1, 1.0, 0.0), axis=1, keepdims=True)
    again_r = jnp.sum(jnp.where(partner_1c == partner_0, 1.0, 0.0), axis=0, keepdims=True)
    partner_col = jnp.concatenate([jnp.where(again_c > 0.0, -1.0, partner_0c), partner_1c], axis=0)
    partner_row = jnp.concatenate([jnp.where(again_r > 0.0, -1.0, partner_0), partner_1], axis=1)
    partner_col = jnp.where(partner_col < 2 * tile, -1.0, partner_col)
    partner_row = jnp.where(partner_row < 2 * tile, -1.0, partner_row)
    columns = lax.broadcasted_iota(jnp.int32, (tile, tile), 1).astype(F32)
    depths = lax.broadcasted_iota(jnp.int32, (tile, tile), 0).astype(F32)
    across = lax.broadcasted_iota(jnp.int32, (3 * tile, tile), 1).astype(F32)

    def first_of(index):
        return (index * tile).astype(F32)

    loads[4].wait()
    taken = jnp.zeros((3 * tile, tile), F32)
    for n in range(x_n):
        hit = (source - first_of(r + rows_n * n)) == across
        mark = jnp.where(hit, 1.0, 0.0).astype(BF)
        block = halves(kkt[n * tile : (n + 1) * tile, :])
        taken = taken + dot_n(mark, block[0], NN) + dot_n(mark, block[1], NN)
    for n in range(y_n):
        for core in range(2):
            q = 2 * n + core
            for part in range(3):
                picked[core, n, part * width : (part + 1) * width, :] = taken[
                    part * tile + q * width : part * tile + (q + 1) * width
                ]

    pl.semaphore_wait(barrier, 2 * y_n + z_n + x_n - 3)

    def chip_copy(d):
        n = lax.rem(y + d, y_n)
        return remote(picked.at[1 - k, n], near_in.at[d], p_send.at[d], p_recv.at[d], twin)

    cut = 3 * width // 2

    def y_copy(d, half):
        part = pl.ds(half * cut, cut)
        return remote(
            chip_sum.at[d - 1, part],
            far_in.at[d - 1, part],
            r_send.at[half, d - 1],
            r_recv.at[half, d - 1],
            y_peer(d),
        )

    order = [2, 1, 3, 0] if y_n == 4 else list(range(1, y_n)) + [0]
    for d in order:
        chip_copy(d).start()
    for d in order[:-1]:
        chip_copy(d).wait_recv()
        chip_sum[d - 1] = picked[k, lax.rem(y + d, y_n)] + near_in[d]
        y_copy(d, 0).start()
    for d in order[:-1]:
        y_copy(d, 1).start()
    loads[5].wait()
    inv0 = halves(inverses[0].T)
    inv1 = halves(inverses[1].T)
    chip_copy(0).wait_recv()

    def gather_copy(ref, d, send, recv):
        return remote(ref.at[r], ref.at[r], send.at[d - 1], recv.at[d - 1], y_peer(d))

    def gathered(ref, d, send, recv):
        q = owner(d, 0)
        return remote(ref.at[q], ref.at[q], send.at[d - 1], recv.at[d - 1], y_peer(d))

    def twin_copy(ref, d, flip, send, recv):
        q = owner(d, flip)
        return remote(ref.at[q], ref.at[q], send.at[d], recv.at[d], twin)

    offset = lax.rem(z - r + z_n, z_n)
    half = z_n // 2
    is_root = offset == 0
    not_root = jnp.logical_not(is_root)
    upward = offset <= half
    passes = ((offset > 0) & (offset < half)) | (offset > half + 1)
    ahead = jnp.where(upward, 1, z_n - 1)
    reach = jnp.minimum(offset, z_n - offset)
    is_near = reach <= 1
    is_mid = reach == 2
    is_far = reach > 2
    if y_n == 4:
        turn = [(0, 0), (0, 1), (1, 0), (3, 0), (1, 1), (3, 1), (2, 0), (2, 1)]
    else:
        turn = [(d, flip) for d in range(y_n) for flip in range(2)]
    spans = []
    for e in range(rows_n):
        count_e = 4 if e in (0, rows_n - 1) else 2
        depth_e = 3 * width // count_e
        spans += [(e, n * depth_e, depth_e) for n in range(count_e)]
    pieces = len(spans)

    def spot(i):
        e, start, size = spans[i]
        return owner(*turn[e]), pl.ds(start, size)

    def z_copy(src, i, slot, step):
        q, part = spot(i)
        return remote(
            src.at[q, part], wide.at[x, q, part], z_send.at[slot, i], z_recv.at[i], z_peer(step)
        )

    def x_copy(src, i, side):
        q, part = spot(i)
        return remote(
            src.at[q, part],
            wide.at[x, q, part],
            x_send.at[side, i],
            x_recv.at[side, i],
            x_peer(1 if side == 0 else x_n - 1),
        )

    def f_copy(i):
        q, part = spot(i)
        step = 1 if i % 2 == 0 else x_n - 1
        held = wide.at[lax.rem(x + x_n - step, x_n), q, part]
        return remote(held, held, f_send.at[i], f_recv.at[i], x_peer(step))

    def own_piece(i):
        q, part = spot(i)
        d, flip = turn[spans[i][0]]

        @pl.when(is_root)
        def _():
            if spans[i][1] == 0 and flip == 1:
                twin_copy(strip, d, 1, h_send, h_recv).wait_recv()
            z_copy(strip, i, 0, 1).start()
            z_copy(strip, i, 1, z_n - 1).start()
            x_copy(strip, i, 0).start()
            x_copy(strip, i, 1).start()
            wide[x, q, part] = strip[q, part]

        @pl.when(not_root)
        def _():
            z_copy(wide.at[x], i, 0, ahead).wait_recv()

            @pl.when(passes)
            def _():
                z_copy(wide.at[x], i, 0, ahead).start()

            x_copy(wide.at[x], i, 0).start()
            x_copy(wide.at[x], i, 1).start()

    def side_piece(i):
        for side in (i % 2, 1 - i % 2):
            x_copy(wide.at[x], i, side).wait_recv()
            if side == i % 2:
                f_copy(i).start()

    def share_copy(d):
        return remote(
            shares.at[lax.rem(z + d, z_n)],
            share_in.at[d - 1],
            cz_send.at[d - 1],
            cz_recv.at[d - 1],
            z_peer(d),
        )

    def cross_copy(d):
        return remote(share, cross.at[d - 1], cx_send.at[d - 1], cx_recv.at[d - 1], x_peer(d))

    def share_back(d):
        return remote(
            summed.at[z], summed.at[z], cg_send.at[d - 1], cg_recv.at[d - 1], z_peer(d)
        )

    def share_taken(d):
        q = lax.rem(z - d + z_n, z_n)
        return remote(
            summed.at[q], summed.at[q], cg_send.at[d - 1], cg_recv.at[d - 1], z_peer(d)
        )

    def corner_z():
        value = shares[z]
        for d in range(1, z_n):
            share_copy(d).wait_recv()
            value = value + share_in[d - 1]
        share[...] = value
        for d in range(1, x_n):
            cross_copy(d).start()

    def corner_x():
        value = share[...]
        for d in range(1, x_n):
            cross_copy(d).wait_recv()
            value = value + cross[d - 1]
        summed[z] = value
        for d in range(1, z_n):
            share_back(d).start()

    def corner_back():
        for d in range(1, z_n):
            share_taken(d).wait_recv()
        flat = jnp.concatenate([summed[n] for n in range(z_n)], axis=0)
        corner[r] = flat[: 4 * width]
        special[r] = flat[4 * width :]
        for d in range(1, y_n):
            gather_copy(corner, d, cr_send, cr_recv).start()
        twin_copy(corner, 0, 0, ch_send, ch_recv).start()
        for home in range(2):
            @pl.when((x == 0) & (z == home) & (r != home))
            def _():
                remote(
                    special.at[r], special.at[r], sp_send, sp_recv.at[r], (home, x, z)
                ).start()

    def corner_twin():
        for d in range(1, y_n):
            gathered(corner, d, cr_send, cr_recv).wait_recv()
            twin_copy(corner, d, 0, ch_send, ch_recv).start()

    steps = [corner_z, corner_x, corner_back, corner_twin]
    spots = [[5, 7, 13, 15], [3, 5, 11, 15], [-1, -1, 8, 13]]
    if y_n != 4:
        spots = [[2, 3, 5, 6]] * 3

    def corner_steps(i):
        for kind, at in zip((is_near, is_mid, is_far), spots):
            if i in at:

                @pl.when(kind)
                def _():
                    for step, place in zip(steps, at):
                        if place == i:
                            step()

    for half in range(2):
        rows_h = slice(half * cut, (half + 1) * cut)
        total = picked[k, y, rows_h, :] + near_in[0, rows_h, :]
        for d in range(1, y_n):
            y_copy(d, half).wait_recv()
            total = total + far_in[d - 1, rows_h, :]
        strip[r, rows_h, :] = total

        @pl.when(is_root)
        def _():
            for i in (2 * half, 2 * half + 1):
                q, part = spot(i)
                z_copy(strip, i, 0, 1).start()
                z_copy(strip, i, 1, z_n - 1).start()
                x_copy(strip, i, 0).start()
                x_copy(strip, i, 1).start()
                wide[x, q, part] = strip[q, part]

    for d in range(1, y_n):
        gather_copy(strip, d, g_send, g_recv).start()
    twin_copy(strip, 0, 0, h_send, h_recv).start()

    moves = jnp.where((source - first_of(c)) == across, 1.0, 0.0).astype(BF)
    piece = halves(strip[r])
    part = dot_n(piece[0], moves, NT) + dot_n(piece[1], moves, NT)
    blocks = ((0, 2), (1, 2), (2, 2), (0, 1), (0, 0), (1, 1))
    stacked = jnp.concatenate(
        [
            part[i * width : (i + 1) * width, j * tile : (j + 1) * tile]
            for i, j in blocks
        ],
        axis=0,
    )
    depth = 6 * width // z_n
    for n in range(z_n):
        shares[n] = stacked[n * depth : (n + 1) * depth]
    for d in range(1, z_n):
        share_copy(d).start()

    for d in (1, 3, 2) if y_n == 4 else range(1, y_n):
        gathered(strip, d, g_send, g_recv).wait_recv()
        twin_copy(strip, d, 0, h_send, h_recv).start()

    corner_steps(-1)
    lag = 5
    for i in range(pieces):
        if i > 3:
            own_piece(i)
        else:

            @pl.when(not_root)
            def _():
                z_copy(wide.at[x], i, 0, ahead).wait_recv()

                @pl.when(passes)
                def _():
                    z_copy(wide.at[x], i, 0, ahead).start()

                x_copy(wide.at[x], i, 0).start()
                x_copy(wide.at[x], i, 1).start()

        corner_steps(i)
        if i >= lag:
            side_piece(i - lag)
    for d in range(y_n):
        twin_copy(corner, d, 1, ch_send, ch_recv).wait_recv()

        @pl.when(not_root)
        def _():
            twin_copy(strip, d, 1, h_send, h_recv).wait_recv()

    def along_d(lower_t, panel):
        pivot = table[:, panel : panel + 1]
        after = table[:, 2 + panel : 3 + panel]
        before = table[:, 4 + panel : 5 + panel]
        return (
            lower_t * pivot
            + pltpu.roll(lower_t, tile - 1, 0) * after
            + pltpu.roll(lower_t, 1, 0) * before
        )

    def rows_of(ref, part):
        return jnp.concatenate(
            [ref[q, part * width : (part + 1) * width, :] for q in range(rows_n)], axis=0
        )

    block_01 = rows_of(corner, 3)
    low0_1 = dot3(inv0, halves(block_01))
    scaled0_1 = along_d(low0_1, 0)
    scaled0_1_rows = halves(scaled0_1.T)
    to_partner = [halves(rows_of(corner, part)) for part in range(3)]

    def panels(ref, index):
        hit = (partner_col - first_of(index)) == columns
        mark = jnp.where(hit, 1.0, 0.0).astype(BF)
        keep = 1.0 - jnp.sum(jnp.where(hit, 1.0, 0.0), axis=0, keepdims=True)
        fixed = [
            rows_of(ref, part) * keep
            + dot_n(to_partner[part][0], mark, NN)
            + dot_n(to_partner[part][1], mark, NN)
            for part in range(3)
        ]
        upper = jnp.where(index == 1, block_01, fixed[0])
        low0 = dot3(inv0, halves(upper)) * jnp.where(index > 0, 1.0, 0.0)
        below = fixed[1] - dot3(scaled0_1_rows, halves(low0))
        low1 = dot3(inv1, halves(below)) * jnp.where(index > 1, 1.0, 0.0)
        return low0, low1, fixed[2], mark, keep

    low0_c, low1_c, moved_c, mark_c, keep_c = panels(strip, c)
    scaled0 = along_d(low0_c, 0)
    scaled1 = along_d(low1_c, 1)
    scaled0_rows = halves(scaled0.T)
    scaled1_rows = halves(scaled1.T)
    moved_rows = halves(moved_c.T)
    hit_c = (partner_row - first_of(c)) == depths
    mark_rows = jnp.where(hit_c, 1.0, 0.0).astype(BF)

    def slot_rows(slot):
        index = r + rows_n * slot
        low0, low1, moved, mark, keep = panels(wide.at[slot], index)
        place = pl.ds(pl.multiple_of(slot * tile, tile), tile)

        @pl.when(c > 1)
        def _():
            hit = (partner_row - first_of(index)) == depths
            keep_rows = 1.0 - jnp.sum(jnp.where(hit, 1.0, 0.0), axis=1, keepdims=True)
            moved_h = halves(moved * keep)
            change = dot_n(moved_rows[0], mark, NN) + dot_n(moved_rows[1], mark, NN)
            change = change + dot_n(mark_rows, moved_h[0], NN) + dot_n(mark_rows, moved_h[1], NN)
            change = change - dot3(scaled0_rows, halves(low0))
            change = change - dot3(scaled1_rows, halves(low1))
            value = kkt[place, :] * keep_rows * keep_c + change.T
            out[place, :] = jnp.where(
                index == 0, scaled0, jnp.where(index == 1, scaled1, value)
            )

        @pl.when(c == 0)
        def _():
            out[place, :] = jnp.where(index == 0, rows_of(special, 0), low0.T)

        @pl.when(c == 1)
        def _():
            first = rows_of(special, 1) - dot3(scaled0_1_rows, halves(low0_1)).T
            value = jnp.where(index == 1, first, low1.T)
            out[place, :] = jnp.where(index == 0, scaled0_1, value)

    for home in range(2):
        for n in range(rows_n):
            if n != home:

                @pl.when((x == 0) & (z == home) & (r == home))
                def _():
                    remote(
                        special.at[n], special.at[n], sp_send, sp_recv.at[n], (n, x, z)
                    ).wait_recv()

    side_piece(pieces - 5)
    side_piece(pieces - 4)
    slot_rows(x)
    for i in range(pieces - 3, pieces):
        side_piece(i)

    for step in (1, 3):
        slot_rows(lax.rem(x + step, x_n))
    for i in range(pieces):
        f_copy(i).wait()
    slot_rows(lax.rem(x + 2, x_n))

    for d in range(y_n):
        twin_copy(strip, d, 0, h_send, h_recv).wait_send()
        twin_copy(corner, d, 0, ch_send, ch_recv).wait_send()
        chip_copy(d).wait_send()
    for d in range(1, y_n):
        y_copy(d, 0).wait_send()
        y_copy(d, 1).wait_send()
        gather_copy(strip, d, g_send, g_recv).wait_send()
        gather_copy(corner, d, cr_send, cr_recv).wait_send()
    for i in range(pieces):
        x_copy(wide.at[x], i, 0).wait_send()
        x_copy(wide.at[x], i, 1).wait_send()

        @pl.when(is_root | passes)
        def _():
            z_copy(wide.at[x], i, 0, ahead).wait_send()

        @pl.when(is_root)
        def _():
            z_copy(wide.at[x], i, 1, ahead).wait_send()

    for d in range(1, z_n):
        share_copy(d).wait_send()
        share_back(d).wait_send()
    for d in range(1, x_n):
        cross_copy(d).wait_send()
    for home in range(2):
        for n in range(rows_n):
            if n != home:
                here = (x == 0) & (z == home)

                @pl.when(here & (r == n))
                def _():
                    remote(
                        special.at[n], special.at[n], sp_send, sp_recv.at[n], (home, x, z)
                    ).wait_send()


def shards(kkt, swaps, inverses, pivots, couplings, pattern):
    tile = inverses.shape[1]
    rows_n = lax.axis_size("row")
    x_n = lax.axis_size("col_0")
    z_n = lax.axis_size("col_1")
    y_n = rows_n // 2
    width = tile // rows_n
    depth = 6 * width // z_n
    dma = pltpu.SemaphoreType.DMA
    vmem = pl.BlockSpec(memory_space=pltpu.VMEM)
    return pl.pallas_call(
        functools.partial(step_kernel, (y_n, x_n, z_n, width)),
        out_shape=jax.ShapeDtypeStruct(kkt.shape, F32),
        in_specs=[pl.BlockSpec(memory_space=pltpu.HBM)] * 6,
        out_specs=vmem,
        scratch_shapes=[
            pltpu.VMEM(kkt.shape, F32),
            pltpu.VMEM((4, tile // 2), jnp.int32),
            pltpu.VMEM(inverses.shape, F32),
            pltpu.VMEM(pivots.shape, F32),
            pltpu.VMEM(couplings.shape, F32),
            pltpu.VMEM(pattern.shape, jnp.int32),
            dma((6,)),
            pltpu.VMEM((128, tile), F32),
            pltpu.VMEM((2, y_n, 3 * width, tile), F32),
            pltpu.VMEM((rows_n, 3 * width, tile), F32),
            pltpu.VMEM((x_n, rows_n, 3 * width, tile), F32),
            pltpu.VMEM((rows_n, 4 * width, tile), F32),
            pltpu.VMEM((rows_n, 2 * width, tile), F32),
            pltpu.VMEM((y_n, 3 * width, tile), F32),
            pltpu.VMEM((y_n - 1, 3 * width, tile), F32),
            pltpu.VMEM((y_n - 1, 3 * width, tile), F32),
            pltpu.VMEM((z_n, depth, tile), F32),
            pltpu.VMEM((depth, tile), F32),
            pltpu.VMEM((z_n - 1, depth, tile), F32),
            pltpu.VMEM((x_n - 1, depth, tile), F32),
            pltpu.VMEM((z_n, depth, tile), F32),
            dma((y_n,)),
            dma((y_n,)),
            dma((2, y_n - 1)),
            dma((2, y_n - 1)),
            dma((y_n - 1,)),
            dma((y_n - 1,)),
            dma((y_n,)),
            dma((y_n,)),
            dma((2, 2 * rows_n + 4)),
            dma((2 * rows_n + 4,)),
            dma((2, 2 * rows_n + 4)),
            dma((2, 2 * rows_n + 4)),
            dma((2 * rows_n + 4,)),
            dma((2 * rows_n + 4,)),
            dma((z_n - 1,)),
            dma((z_n - 1,)),
            dma((x_n - 1,)),
            dma((x_n - 1,)),
            dma((z_n - 1,)),
            dma((z_n - 1,)),
            dma((y_n - 1,)),
            dma((y_n - 1,)),
            dma((y_n,)),
            dma((y_n,)),
            dma,
            dma((rows_n,)),
        ],
        compiler_params=pltpu.CompilerParams(collective_id=0, has_side_effects=True),
    )(kkt, swaps.reshape(4, -1), inverses, pivots, couplings, pattern)


def solution(mesh):
    z_size = mesh.shape["row"]
    finer = Mesh(mesh.devices.reshape(mesh.shape["row"], -1, z_size), ("row", "col_0", "col_1"))
    in_specs = (P("row", COL), P(), P(), P(), P(), P())
    return jax.shard_map(
        shards, mesh=finer, in_specs=in_specs, out_specs=P("row", COL), check_vma=False
    )
```

```python
import functools

import jax
import jax.numpy as jnp
from jax import lax
from jax.experimental import pallas as pl
from jax.experimental.pallas import tpu as pltpu
from jax.sharding import Mesh
from jax.sharding import PartitionSpec as P

COL = ("col_0", "col_1")
BF = jnp.bfloat16
F32 = jnp.float32
NN = ((1,), (0,))
NT = ((1,), (1,))


def halves(a):
    high = a.astype(BF)
    return high, (a - high.astype(F32)).astype(BF)


def dot_n(a, b, dims):
    return lax.dot_general(a, b, (dims, ((), ())), preferred_element_type=F32)


def dot3(a, b):
    return dot_n(a[0], b[0], NN) + (dot_n(a[0], b[1], NN) + dot_n(a[1], b[0], NN))


def swapped(rows, lead, partner):
    to_partner = rows == lead
    to_lead = rows == partner
    moved = jnp.where(to_partner, partner, 0.0) + jnp.where(to_lead, lead, 0.0)
    touched = jnp.where(to_partner | to_lead, 1.0, 0.0)
    moved = jnp.sum(moved, axis=1, keepdims=True)
    return jnp.where(jnp.sum(touched, axis=1, keepdims=True) > 0.0, moved, rows)


MESH = pl.DeviceIdType.MESH


def remote(src, dst, send, recv, device):
    return pltpu.make_async_remote_copy(
        src_ref=src, dst_ref=dst, send_sem=send, recv_sem=recv, device_id=device, device_id_type=MESH
    )


def step_kernel(
    sizes,
    kkt_hbm,
    swaps_hbm,
    inverses_hbm,
    pivots_hbm,
    couplings_hbm,
    pattern_hbm,
    out,
    kkt,
    swaps,
    inverses,
    pivots,
    couplings,
    pattern,
    in_sem,
    coef,
    picked,
    strip,
    wide,
    corner,
    special,
    near_in,
    chip_sum,
    far_in,
    shares,
    share,
    share_in,
    cross,
    summed,
    p_send,
    p_recv,
    r_send,
    r_recv,
    g_send,
    g_recv,
    h_send,
    h_recv,
    z_send,
    z_recv,
    x_send,
    x_recv,
    f_send,
    f_recv,
    cz_send,
    cz_recv,
    cx_send,
    cx_recv,
    cg_send,
    cg_recv,
    cr_send,
    cr_recv,
    ch_send,
    ch_recv,
    sp_send,
    sp_recv,
):
    y_n, x_n, z_n, width = sizes
    rows_n = 2 * y_n
    r = lax.axis_index("row")
    x = lax.axis_index("col_0")
    z = lax.axis_index("col_1")
    y = r // 2
    k = lax.rem(r, 2)
    twin = (r + 1 - 2 * k, x, z)

    def y_peer(d):
        return (lax.rem(r + 2 * d, rows_n), x, z)

    def z_peer(d):
        return (r, x, lax.rem(z + d + z_n, z_n))

    def x_peer(d):
        return (r, lax.rem(x + d + x_n, x_n), z)

    def owner(d, flip):
        core = k if flip == 0 else 1 - k
        return 2 * lax.rem(y - d + y_n, y_n) + core

    loads = [
        pltpu.make_async_copy(src, dst, in_sem.at[n])
        for n, (src, dst) in enumerate(
            (
                (swaps_hbm, swaps),
                (pivots_hbm, pivots),
                (couplings_hbm, couplings),
                (pattern_hbm, pattern),
                (kkt_hbm, kkt),
                (inverses_hbm, inverses),
            )
        )
    ]
    for load in loads:
        load.start()
    barrier = pltpu.get_barrier_semaphore()
    pl.semaphore_signal(barrier, inc=1, device_id=twin, device_id_type=MESH)
    for d in range(1, y_n):
        pl.semaphore_signal(barrier, inc=1, device_id=y_peer(d), device_id_type=MESH)
    for d in range(1, z_n):
        pl.semaphore_signal(barrier, inc=1, device_id=z_peer(d), device_id_type=MESH)
    for d in range(1, x_n):
        pl.semaphore_signal(barrier, inc=1, device_id=x_peer(d), device_id_type=MESH)
    for d in range(1, y_n):
        there = (2 * lax.rem(y + d, y_n) + 1 - k, x, z)
        pl.semaphore_signal(barrier, inc=1, device_id=there, device_id_type=MESH)

    c = x * z_n + z
    tile = inverses.shape[1]
    for load in loads[:4]:
        load.wait()
    count = tile // 2
    lanes = lax.broadcasted_iota(jnp.int32, (2, tile), 1)
    links = couplings[...] * pattern[...].astype(F32)
    links = jnp.where(lanes == tile - 1, 0.0, links)
    swap_rows = swaps[...].astype(F32)
    coef[...] = jnp.zeros_like(coef)
    coef[0:2, :] = pivots[...]
    coef[2:4, :] = links
    coef[4:6, :] = jnp.where(lanes == 0, 0.0, pltpu.roll(links, 1, 1))
    coef[8:12, 0:count] = swap_rows
    table = coef[...].T
    lead_0, partner_0 = swap_rows[0:1], swap_rows[1:2]
    lead_1, partner_1 = swap_rows[2:3], swap_rows[3:4]
    partner_0c, partner_1c = table[:count, 9:10], table[:count, 11:12]
    top = lax.broadcasted_iota(jnp.int32, (2 * tile, 1), 0).astype(F32)
    rows = jnp.concatenate([top, partner_0c, partner_1c], axis=0)
    source = swapped(swapped(rows, lead_1, partner_1), lead_0, partner_0)
    again_c = jnp.sum(jnp.where(partner_0c == partner_1, 1.0, 0.0), axis=1, keepdims=True)
    again_r = jnp.sum(jnp.where(partner_1c == partner_0, 1.0, 0.0), axis=0, keepdims=True)
    partner_col = jnp.concatenate([jnp.where(again_c > 0.0, -1.0, partner_0c), partner_1c], axis=0)
    partner_row = jnp.concatenate([jnp.where(again_r > 0.0, -1.0, partner_0), partner_1], axis=1)
    partner_col = jnp.where(partner_col < 2 * tile, -1.0, partner_col)
    partner_row = jnp.where(partner_row < 2 * tile, -1.0, partner_row)
    columns = lax.broadcasted_iota(jnp.int32, (tile, tile), 1).astype(F32)
    depths = lax.broadcasted_iota(jnp.int32, (tile, tile), 0).astype(F32)
    across = lax.broadcasted_iota(jnp.int32, (3 * tile, tile), 1).astype(F32)

    def first_of(index):
        return (index * tile).astype(F32)

    loads[4].wait()
    taken = jnp.zeros((3 * tile, tile), F32)
    for n in range(x_n):
        hit = (source - first_of(r + rows_n * n)) == across
        mark = jnp.where(hit, 1.0, 0.0).astype(BF)
        block = halves(kkt[n * tile : (n + 1) * tile, :])
        taken = taken + dot_n(mark, block[0], NN) + dot_n(mark, block[1], NN)
    for n in range(y_n):
        for core in range(2):
            q = 2 * n + core
            for part in range(3):
                picked[core, n, part * width : (part + 1) * width, :] = taken[
                    part * tile + q * width : part * tile + (q + 1) * width
                ]

    pl.semaphore_wait(barrier, 2 * y_n + z_n + x_n - 3)

    def chip_copy(d):
        n = lax.rem(y + d, y_n)
        return remote(picked.at[1 - k, n], near_in.at[d], p_send.at[d], p_recv.at[d], twin)

    cut = 3 * width // 2

    def y_copy(d, half):
        part = pl.ds(half * cut, cut)
        return remote(
            chip_sum.at[d - 1, part],
            far_in.at[d - 1, part],
            r_send.at[half, d - 1],
            r_recv.at[half, d - 1],
            y_peer(d),
        )

    order = [2, 1, 3, 0] if y_n == 4 else list(range(1, y_n)) + [0]
    for d in order:
        chip_copy(d).start()
    for d in order[:-1]:
        chip_copy(d).wait_recv()
        chip_sum[d - 1] = picked[k, lax.rem(y + d, y_n)] + near_in[d]
        y_copy(d, 0).start()
    for d in order[:-1]:
        y_copy(d, 1).start()
    loads[5].wait()
    inv0 = halves(inverses[0].T)
    inv1 = halves(inverses[1].T)
    chip_copy(0).wait_recv()

    def gather_copy(ref, d, send, recv):
        return remote(ref.at[r], ref.at[r], send.at[d - 1], recv.at[d - 1], y_peer(d))

    def gathered(ref, d, send, recv):
        q = owner(d, 0)
        return remote(ref.at[q], ref.at[q], send.at[d - 1], recv.at[d - 1], y_peer(d))

    def twin_copy(ref, d, flip, send, recv):
        q = owner(d, flip)
        return remote(ref.at[q], ref.at[q], send.at[d], recv.at[d], twin)

    offset = lax.rem(z - r + z_n, z_n)
    half = z_n // 2
    is_root = offset == 0
    not_root = jnp.logical_not(is_root)
    upward = offset <= half
    passes = ((offset > 0) & (offset < half)) | (offset > half + 1)
    ahead = jnp.where(upward, 1, z_n - 1)
    reach = jnp.minimum(offset, z_n - offset)
    is_near = reach <= 1
    is_mid = reach == 2
    is_far = reach > 2
    if y_n == 4:
        turn = [(0, 0), (0, 1), (1, 0), (3, 0), (1, 1), (3, 1), (2, 0), (2, 1)]
    else:
        turn = [(d, flip) for d in range(y_n) for flip in range(2)]
    spans = []
    for e in range(rows_n):
        count_e = 4 if e in (0, rows_n - 1) else 2
        depth_e = 3 * width // count_e
        spans += [(e, n * depth_e, depth_e) for n in range(count_e)]
    pieces = len(spans)

    def spot(i):
        e, start, size = spans[i]
        return owner(*turn[e]), pl.ds(start, size)

    def z_copy(src, i, slot, step):
        q, part = spot(i)
        return remote(
            src.at[q, part], wide.at[x, q, part], z_send.at[slot, i], z_recv.at[i], z_peer(step)
        )

    def x_copy(src, i, side):
        q, part = spot(i)
        return remote(
            src.at[q, part],
            wide.at[x, q, part],
            x_send.at[side, i],
            x_recv.at[side, i],
            x_peer(1 if side == 0 else x_n - 1),
        )

    def f_copy(i):
        q, part = spot(i)
        step = 1 if i % 2 == 0 else x_n - 1
        held = wide.at[lax.rem(x + x_n - step, x_n), q, part]
        return remote(held, held, f_send.at[i], f_recv.at[i], x_peer(step))

    def own_piece(i):
        q, part = spot(i)
        d, flip = turn[spans[i][0]]

        @pl.when(is_root)
        def _():
            if spans[i][1] == 0 and flip == 1:
                twin_copy(strip, d, 1, h_send, h_recv).wait_recv()
            z_copy(strip, i, 0, 1).start()
            z_copy(strip, i, 1, z_n - 1).start()
            x_copy(strip, i, 0).start()
            x_copy(strip, i, 1).start()
            wide[x, q, part] = strip[q, part]

        @pl.when(not_root)
        def _():
            z_copy(wide.at[x], i, 0, ahead).wait_recv()

            @pl.when(passes)
            def _():
                z_copy(wide.at[x], i, 0, ahead).start()

            x_copy(wide.at[x], i, 0).start()
            x_copy(wide.at[x], i, 1).start()

    def side_piece(i):
        for side in (i % 2, 1 - i % 2):
            x_copy(wide.at[x], i, side).wait_recv()
            if side == i % 2:
                f_copy(i).start()

    def share_copy(d):
        return remote(
            shares.at[lax.rem(z + d, z_n)],
            share_in.at[d - 1],
            cz_send.at[d - 1],
            cz_recv.at[d - 1],
            z_peer(d),
        )

    def cross_copy(d):
        return remote(share, cross.at[d - 1], cx_send.at[d - 1], cx_recv.at[d - 1], x_peer(d))

    def share_back(d):
        return remote(
            summed.at[z], summed.at[z], cg_send.at[d - 1], cg_recv.at[d - 1], z_peer(d)
        )

    def share_taken(d):
        q = lax.rem(z - d + z_n, z_n)
        return remote(
            summed.at[q], summed.at[q], cg_send.at[d - 1], cg_recv.at[d - 1], z_peer(d)
        )

    def corner_z():
        value = shares[z]
        for d in range(1, z_n):
            share_copy(d).wait_recv()
            value = value + share_in[d - 1]
        share[...] = value
        for d in range(1, x_n):
            cross_copy(d).start()

    def corner_x():
        value = share[...]
        for d in range(1, x_n):
            cross_copy(d).wait_recv()
            value = value + cross[d - 1]
        summed[z] = value
        for d in range(1, z_n):
            share_back(d).start()

    def corner_back():
        for d in range(1, z_n):
            share_taken(d).wait_recv()
        flat = jnp.concatenate([summed[n] for n in range(z_n)], axis=0)
        corner[r] = flat[: 4 * width]
        special[r] = flat[4 * width :]
        for d in range(1, y_n):
            gather_copy(corner, d, cr_send, cr_recv).start()
        twin_copy(corner, 0, 0, ch_send, ch_recv).start()
        for home in range(2):
            @pl.when((x == 0) & (z == home) & (r != home))
            def _():
                remote(
                    special.at[r], special.at[r], sp_send, sp_recv.at[r], (home, x, z)
                ).start()

    def corner_twin():
        for d in range(1, y_n):
            gathered(corner, d, cr_send, cr_recv).wait_recv()
            twin_copy(corner, d, 0, ch_send, ch_recv).start()

    steps = [corner_z, corner_x, corner_back, corner_twin]
    spots = [[5, 7, 13, 15], [3, 5, 11, 15], [3, 5, 9, 13]]
    if y_n != 4:
        spots = [[2, 3, 5, 6]] * 3

    def corner_steps(i):
        for kind, at in zip((is_near, is_mid, is_far), spots):
            if i in at:

                @pl.when(kind)
                def _():
                    for step, place in zip(steps, at):
                        if place == i:
                            step()

    for half in range(2):
        rows_h = slice(half * cut, (half + 1) * cut)
        total = picked[k, y, rows_h, :] + near_in[0, rows_h, :]
        for d in range(1, y_n):
            y_copy(d, half).wait_recv()
            total = total + far_in[d - 1, rows_h, :]
        strip[r, rows_h, :] = total

        @pl.when(is_root)
        def _():
            for i in (2 * half, 2 * half + 1):
                q, part = spot(i)
                z_copy(strip, i, 0, 1).start()
                z_copy(strip, i, 1, z_n - 1).start()
                x_copy(strip, i, 0).start()
                x_copy(strip, i, 1).start()
                wide[x, q, part] = strip[q, part]

    for d in range(1, y_n):
        gather_copy(strip, d, g_send, g_recv).start()
    twin_copy(strip, 0, 0, h_send, h_recv).start()

    moves = jnp.where((source - first_of(c)) == across, 1.0, 0.0).astype(BF)
    piece = halves(strip[r])
    part = dot_n(piece[0], moves, NT) + dot_n(piece[1], moves, NT)
    blocks = ((0, 2), (1, 2), (2, 2), (0, 1), (0, 0), (1, 1))
    stacked = jnp.concatenate(
        [
            part[i * width : (i + 1) * width, j * tile : (j + 1) * tile]
            for i, j in blocks
        ],
        axis=0,
    )
    depth = 6 * width // z_n
    for n in range(z_n):
        shares[n] = stacked[n * depth : (n + 1) * depth]
    for d in range(1, z_n):
        share_copy(d).start()

    def pass_on(i):
        z_copy(wide.at[x], i, 0, ahead).wait_recv()

        @pl.when(passes)
        def _():
            z_copy(wide.at[x], i, 0, ahead).start()

        x_copy(wide.at[x], i, 0).start()
        x_copy(wide.at[x], i, 1).start()

    @pl.when(not_root & (reach <= 2))
    def _():
        for i in range(4):
            pass_on(i)

    for d in (1, 3, 2) if y_n == 4 else range(1, y_n):
        gathered(strip, d, g_send, g_recv).wait_recv()
        twin_copy(strip, d, 0, h_send, h_recv).start()

    lag = 5
    for i in range(pieces):
        if i > 3:
            own_piece(i)
        else:

            @pl.when(reach > 2)
            def _():
                pass_on(i)

        corner_steps(i)
        if i >= lag:
            side_piece(i - lag)
    for d in range(y_n):
        twin_copy(corner, d, 1, ch_send, ch_recv).wait_recv()

        @pl.when(not_root)
        def _():
            twin_copy(strip, d, 1, h_send, h_recv).wait_recv()

    def along_d(lower_t, panel):
        pivot = table[:, panel : panel + 1]
        after = table[:, 2 + panel : 3 + panel]
        before = table[:, 4 + panel : 5 + panel]
        return (
            lower_t * pivot
            + pltpu.roll(lower_t, tile - 1, 0) * after
            + pltpu.roll(lower_t, 1, 0) * before
        )

    def rows_of(ref, part):
        return jnp.concatenate(
            [ref[q, part * width : (part + 1) * width, :] for q in range(rows_n)], axis=0
        )

    block_01 = rows_of(corner, 3)
    low0_1 = dot3(inv0, halves(block_01))
    scaled0_1 = along_d(low0_1, 0)
    scaled0_1_rows = halves(scaled0_1.T)
    to_partner = [halves(rows_of(corner, part)) for part in range(3)]

    def panels(ref, index):
        hit = (partner_col - first_of(index)) == columns
        mark = jnp.where(hit, 1.0, 0.0).astype(BF)
        keep = 1.0 - jnp.sum(jnp.where(hit, 1.0, 0.0), axis=0, keepdims=True)
        fixed = [
            rows_of(ref, part) * keep
            + dot_n(to_partner[part][0], mark, NN)
            + dot_n(to_partner[part][1], mark, NN)
            for part in range(3)
        ]
        upper = jnp.where(index == 1, block_01, fixed[0])
        low0 = dot3(inv0, halves(upper)) * jnp.where(index > 0, 1.0, 0.0)
        below = fixed[1] - dot3(scaled0_1_rows, halves(low0))
        low1 = dot3(inv1, halves(below)) * jnp.where(index > 1, 1.0, 0.0)
        return low0, low1, fixed[2], mark, keep

    low0_c, low1_c, moved_c, mark_c, keep_c = panels(strip, c)
    scaled0 = along_d(low0_c, 0)
    scaled1 = along_d(low1_c, 1)
    scaled0_rows = halves(scaled0.T)
    scaled1_rows = halves(scaled1.T)
    moved_rows = halves(moved_c.T)
    hit_c = (partner_row - first_of(c)) == depths
    mark_rows = jnp.where(hit_c, 1.0, 0.0).astype(BF)

    def slot_rows(slot):
        index = r + rows_n * slot
        low0, low1, moved, mark, keep = panels(wide.at[slot], index)
        place = pl.ds(pl.multiple_of(slot * tile, tile), tile)

        @pl.when(c > 1)
        def _():
            hit = (partner_row - first_of(index)) == depths
            keep_rows = 1.0 - jnp.sum(jnp.where(hit, 1.0, 0.0), axis=1, keepdims=True)
            moved_h = halves(moved * keep)
            change = dot_n(moved_rows[0], mark, NN) + dot_n(moved_rows[1], mark, NN)
            change = change + dot_n(mark_rows, moved_h[0], NN) + dot_n(mark_rows, moved_h[1], NN)
            change = change - dot3(scaled0_rows, halves(low0))
            change = change - dot3(scaled1_rows, halves(low1))
            value = kkt[place, :] * keep_rows * keep_c + change.T
            value = jnp.where(index == 0, scaled0, jnp.where(index == 1, scaled1, value))
            out[place, :] = value - kkt[place, :]

        @pl.when(c == 0)
        def _():
            out[place, :] = jnp.where(index == 0, rows_of(special, 0), low0.T) - kkt[place, :]

        @pl.when(c == 1)
        def _():
            first = rows_of(special, 1) - dot3(scaled0_1_rows, halves(low0_1)).T
            value = jnp.where(index == 1, first, low1.T)
            out[place, :] = jnp.where(index == 0, scaled0_1, value) - kkt[place, :]

    for home in range(2):
        for n in range(rows_n):
            if n != home:

                @pl.when((x == 0) & (z == home) & (r == home))
                def _():
                    remote(
                        special.at[n], special.at[n], sp_send, sp_recv.at[n], (n, x, z)
                    ).wait_recv()

    side_piece(pieces - 5)
    side_piece(pieces - 4)
    slot_rows(x)
    for i in range(pieces - 3, pieces):
        side_piece(i)

    for step in (1, 3):
        slot_rows(lax.rem(x + step, x_n))
    for i in range(pieces):
        f_copy(i).wait()
    slot_rows(lax.rem(x + 2, x_n))

    for d in range(y_n):
        twin_copy(strip, d, 0, h_send, h_recv).wait_send()
        twin_copy(corner, d, 0, ch_send, ch_recv).wait_send()
        chip_copy(d).wait_send()
    for d in range(1, y_n):
        y_copy(d, 0).wait_send()
        y_copy(d, 1).wait_send()
        gather_copy(strip, d, g_send, g_recv).wait_send()
        gather_copy(corner, d, cr_send, cr_recv).wait_send()
    for i in range(pieces):
        x_copy(wide.at[x], i, 0).wait_send()
        x_copy(wide.at[x], i, 1).wait_send()

        @pl.when(is_root | passes)
        def _():
            z_copy(wide.at[x], i, 0, ahead).wait_send()

        @pl.when(is_root)
        def _():
            z_copy(wide.at[x], i, 1, ahead).wait_send()

    for d in range(1, z_n):
        share_copy(d).wait_send()
        share_back(d).wait_send()
    for d in range(1, x_n):
        cross_copy(d).wait_send()
    for home in range(2):
        for n in range(rows_n):
            if n != home:
                here = (x == 0) & (z == home)

                @pl.when(here & (r == n))
                def _():
                    remote(
                        special.at[n], special.at[n], sp_send, sp_recv.at[n], (home, x, z)
                    ).wait_send()


def shards(kkt, swaps, inverses, pivots, couplings, pattern):
    tile = inverses.shape[1]
    rows_n = lax.axis_size("row")
    x_n = lax.axis_size("col_0")
    z_n = lax.axis_size("col_1")
    y_n = rows_n // 2
    width = tile // rows_n
    depth = 6 * width // z_n
    dma = pltpu.SemaphoreType.DMA
    vmem = pl.BlockSpec(memory_space=pltpu.VMEM)
    change = pl.pallas_call(
        functools.partial(step_kernel, (y_n, x_n, z_n, width)),
        out_shape=jax.ShapeDtypeStruct(kkt.shape, F32),
        in_specs=[pl.BlockSpec(memory_space=pltpu.HBM)] * 6,
        out_specs=vmem,
        scratch_shapes=[
            pltpu.VMEM(kkt.shape, F32),
            pltpu.VMEM((4, tile // 2), jnp.int32),
            pltpu.VMEM(inverses.shape, F32),
            pltpu.VMEM(pivots.shape, F32),
            pltpu.VMEM(couplings.shape, F32),
            pltpu.VMEM(pattern.shape, jnp.int32),
            dma((6,)),
            pltpu.VMEM((128, tile), F32),
            pltpu.VMEM((2, y_n, 3 * width, tile), F32),
            pltpu.VMEM((rows_n, 3 * width, tile), F32),
            pltpu.VMEM((x_n, rows_n, 3 * width, tile), F32),
            pltpu.VMEM((rows_n, 4 * width, tile), F32),
            pltpu.VMEM((rows_n, 2 * width, tile), F32),
            pltpu.VMEM((y_n, 3 * width, tile), F32),
            pltpu.VMEM((y_n - 1, 3 * width, tile), F32),
            pltpu.VMEM((y_n - 1, 3 * width, tile), F32),
            pltpu.VMEM((z_n, depth, tile), F32),
            pltpu.VMEM((depth, tile), F32),
            pltpu.VMEM((z_n - 1, depth, tile), F32),
            pltpu.VMEM((x_n - 1, depth, tile), F32),
            pltpu.VMEM((z_n, depth, tile), F32),
            dma((y_n,)),
            dma((y_n,)),
            dma((2, y_n - 1)),
            dma((2, y_n - 1)),
            dma((y_n - 1,)),
            dma((y_n - 1,)),
            dma((y_n,)),
            dma((y_n,)),
            dma((2, 2 * rows_n + 4)),
            dma((2 * rows_n + 4,)),
            dma((2, 2 * rows_n + 4)),
            dma((2, 2 * rows_n + 4)),
            dma((2 * rows_n + 4,)),
            dma((2 * rows_n + 4,)),
            dma((z_n - 1,)),
            dma((z_n - 1,)),
            dma((x_n - 1,)),
            dma((x_n - 1,)),
            dma((z_n - 1,)),
            dma((z_n - 1,)),
            dma((y_n - 1,)),
            dma((y_n - 1,)),
            dma((y_n,)),
            dma((y_n,)),
            dma,
            dma((rows_n,)),
        ],
        compiler_params=pltpu.CompilerParams(collective_id=0, has_side_effects=True),
    )(kkt, swaps.reshape(4, -1), inverses, pivots, couplings, pattern)
    return kkt + change


def solution(mesh):
    z_size = mesh.shape["row"]
    finer = Mesh(mesh.devices.reshape(mesh.shape["row"], -1, z_size), ("row", "col_0", "col_1"))
    in_specs = (P("row", COL), P(), P(), P(), P(), P())
    return jax.shard_map(
        shards, mesh=finer, in_specs=in_specs, out_specs=P("row", COL), check_vma=False
    )
```
